256 devices in a mesh: freq: 16 (over x, y_hi, core), tile: 16 (over y_lo, z).
Axes of the slice: x: 4, y: 4 (y_hi: 2, y_lo: 2; y = y_hi * 2 + y_lo), z: 8, core: 2. Of those that a mesh axis runs over, the one named last changes fastest.
Arguments:
- omega: float32 [16], P('freq'), may hold values from 0.2 to 2
- conductivity: float32 [16, 128, 256], P(None, 'tile'), may hold values from 0.1 to 10
- forward_field: float32 [16, 2, 3, 16, 128, 256], P('freq', None, None, None, 'tile'), may hold values from -6 to 6
- adjoint_start: float32 [16, 2, 3, 16, 128, 256], P('freq', None, None, None, 'tile'), may hold values from -6 to 6
- station_data: float32 [16, 2, 2, 8192], P('freq', None, None, 'tile'), may hold values from -6 to 6
- station_owner: int32 [8192, 1], P('tile'), may hold values from 0 to 15; in each aligned block of 512 rows (0 to 511, 512 to 1023, ...) at most 128 rows name the same one
- station_cell: int32 [8192], P('tile'), may hold values from 0 to 2047
Outputs:
- adjoint_field: float32 [16, 2, 3, 16, 128, 256], P('freq', None, None, None, 'tile')
- gradient: float32 [16, 128, 256], P('freq', 'tile')
The draws below stay inside these ranges and needn't reach their ends.
Inputs may be any that keep to these rules, and one draw needn't show every extreme that they name: `station_owner`: among the 512 stations listed on one device, at most 128 have the same owner; some owner gets exactly 128 of them. `station_cell`: counted as x * 256 + y within the owner tile; several stations may share a cell.
All inputs are finite; a program needn't handle non-finite values.
Results may differ from the reference program's by a relative error of at most 0.0003.
Values sent between devices are 32-bit elements; how exact they have to be, the bound alone decides.
No kernel may reach another device: no remote copies, remote signals or barrier semaphores. Data moves between devices by JAX's collectives and lax.ppermute only.
A program may use at most 64 MiB of HBM per device.

```python
import math
import jax
import jax.numpy as jnp
import numpy as np
from jax import lax

CX = 8
NY = 256
NZ = 16
SWEEPS = 4
ST_DEV = 512
CAP = 128
PAIRS = 16
NX = 128
STATIONS = 8192
N_TILE = 16


def set_ends(entries, key, least, high):
    longest = entries.shape.index(max(entries.shape))
    spots = []
    for shift in (0, 1):
        where = [jax.random.randint(jax.random.fold_in(key, axis), (), 0, length) for axis, length in enumerate(entries.shape)]
        where[longest] = (where[longest] + shift) % entries.shape[longest]
        spots.append(tuple(where))
    return entries.at[spots[0]].set(least).at[spots[1]].set(high)


def block_levels(key, extent, split, smallest, high):
    gain = 1.0
    for axis_at, blocks in split:
        draws = jax.random.uniform(jax.random.fold_in(jax.random.fold_in(key, 6), axis_at), (blocks,), jnp.float32, smallest / len(split), high / len(split))
        gain = gain * jnp.repeat(jnp.exp(draws), extent[axis_at] // blocks).reshape((-1,) + (1,) * (len(extent) - 1 - axis_at))
    return gain


def deal_out(key, own, number, rows, count, top, bound, lean):
    order = jax.random.permutation(key, count)
    crowded, usual = load_shares(count, rows * top, bound, lean, True), load_shares(count, rows * top, bound, lean, False)
    places = jnp.arange(count)

    def named(tallies, rotation):
        used = int((tallies > 0).sum())
        fixed = max(1, used // 4)
        shifted = fixed + (places - fixed + rotation * (used - fixed)) % max(1, count - fixed)
        return jnp.zeros((count,), jnp.int32).at[order[jnp.where(places < fixed, places, shifted)]].set(jnp.asarray(tallies, jnp.int32))

    tallies = jnp.where(number % 4 == 0, named(crowded, number // 4), named(usual, number - number // 4 - 1))
    mixed = jax.random.permutation(jax.random.fold_in(own, 3), count)
    source_of, sink = mixed[0:count // 2 * 2:2], mixed[1:count // 2 * 2:2]
    margin = jnp.minimum(tallies[source_of] - 1, bound - tallies[sink]) // 2
    margin = jnp.where((source_of == order[0]) | (sink == order[0]) | (tallies[sink] == 0), 0, jnp.maximum(margin, 0))
    shifted = jax.random.randint(jax.random.fold_in(own, 4), (count // 2,), 0, 1 << 20) % (margin + 1)
    tallies = tallies.at[source_of].add(-shifted).at[sink].add(shifted)
    labels = jnp.searchsorted(jnp.cumsum(tallies), jnp.arange(rows * top), side="right").astype(jnp.int32)
    listing = labels.reshape(top, rows).T
    listing = listing[jax.random.permutation(jax.random.fold_in(own, 1), rows)]
    rotation = jax.random.randint(jax.random.fold_in(own, 2), (rows, 1), 0, top)
    return jnp.take_along_axis(listing, (jnp.arange(top)[None, :] + rotation) % top, axis=1)


def load_shares(number_of, total, limit, lean, full):
    portions = [(1 << 20) // math.isqrt(grade ** lean) + 1 for grade in range(1, number_of + 1)]
    largest = limit if full else min(limit, max(-(-total // number_of), total * portions[0] // sum(portions)))
    least = 1 if total - largest >= number_of - 1 else 0
    given, spare = [largest] + [least] * (number_of - 1), total - largest - least * (number_of - 1)
    while spare > 0:
        movable = [i for i in range(1, number_of) if given[i] < largest] or [i for i in range(1, number_of) if given[i] < limit]
        whole, remaining = sum([portions[i] for i in movable]), spare
        for i in movable:
            addition = min(limit - given[i], max(1, remaining * portions[i] // whole), spare)
            given[i] = given[i] + addition
            spare = spare - addition
    return np.array(given)


def centred(stream_key, dims, spread, reach, cuts=(), kind=jnp.bfloat16):
    result = jax.random.normal(stream_key, dims, jnp.float32) * spread
    if len(cuts) > 0:
        result = block_levels(stream_key, dims, cuts, -0.22, 0.18) * result
    return jnp.clip(result, min=-reach, max=reach).astype(kind)


def setup_inputs(seed: int = 0) -> dict:
    keys = jax.random.split(jax.random.key(seed), 8)
    omega = jnp.clip(jnp.exp(math.log(2.0) - 2.3025851 * jax.random.uniform(keys[0], (PAIRS,), jnp.float32) ** block_levels(keys[0], (PAIRS,), ((0, 16),), -0.2, 0.2)), 0.2, 2.0)
    conductivity = jnp.clip(jnp.exp(math.log(10.0) - 4.6051702 * jax.random.uniform(keys[1], (NZ, NX, NY), jnp.float32) ** block_levels(keys[1], (NZ, NX, NY), ((1, 16),), -0.2, 0.2)), 0.1, 10.0)
    forward_field = centred(keys[2], (PAIRS, 2, 3, NZ, NX, NY), 1.0, 6.0, ((0, 16), (4, 16)), jnp.float32)
    adjoint_start = centred(keys[3], (PAIRS, 2, 3, NZ, NX, NY), 1.0, 6.0, ((0, 16), (4, 16)), jnp.float32)
    station_data = centred(keys[4], (PAIRS, 2, 2, STATIONS), 1.0, 6.0, ((0, 16), (3, 16)), jnp.float32)
    station_owner_keys = jax.random.split(jax.random.fold_in(keys[5], 1), STATIONS // ST_DEV)
    station_owner_turns = jax.random.permutation(jax.random.fold_in(keys[5], 3), STATIONS // ST_DEV)
    station_owner = jax.vmap(lambda own, number: deal_out(jax.random.fold_in(keys[5], 2), own, number, ST_DEV, N_TILE, 1, CAP, 2))(station_owner_keys, station_owner_turns).reshape((STATIONS, 1))
    station_cell = set_ends(jax.random.randint(keys[6], (STATIONS,), 0, CX * NY), jax.random.fold_in(keys[6], 1), 0, (CX * NY) - 1).astype(jnp.int32)
    return dict(omega=omega, conductivity=conductivity, forward_field=forward_field, adjoint_start=adjoint_start, station_data=station_data, station_owner=station_owner, station_cell=station_cell)


penalty = 0.5
damping = 0.7
diagonal_weight = 5.0
unit_steps = ((0, 1, 0), (0, 0, 1), (1, 0, 0))

def offset_view(padded, shift):
    depth = padded.shape[-3] - 2
    across = padded.shape[-2] - 2
    along = padded.shape[-1] - 2
    return padded[..., 1 + shift[0]:1 + shift[0] + depth, 1 + shift[1]:1 + shift[1] + across, 1 + shift[2]:1 + shift[2] + along]

def joined(first_step, second_step, sign_one, sign_two):
    return (sign_one * first_step[0] + sign_two * second_step[0], sign_one * first_step[1] + sign_two * second_step[1], sign_one * first_step[2] + sign_two * second_step[2])

def second_diff(field, target, source):
    step_a = unit_steps[target]
    step_b = unit_steps[source]
    if target == source:
        return offset_view(field, step_a) - 2.0 * offset_view(field, (0, 0, 0)) + offset_view(field, joined(step_a, step_a, -1, 0))
    total = offset_view(field, joined(step_a, step_b, 1, 1)) - offset_view(field, joined(step_a, step_b, 1, -1))
    total = total - offset_view(field, joined(step_a, step_b, -1, 1)) + offset_view(field, joined(step_a, step_b, -1, -1))
    return total / 4.0

def relax(lam_pad, sigma, surface, omega):
    padded = jnp.pad(lam_pad, ((0, 0), (0, 0), (0, 0), (1, 1), (0, 0), (1, 1)))
    components = [padded[:, :, which] for which in range(3)]
    pieces = []
    for target in range(3):
        field = components[target]
        beside_all = jnp.zeros_like(offset_view(field, (0, 0, 0)))
        for step in unit_steps:
            beside_all = beside_all + offset_view(field, step) + offset_view(field, joined(step, step, -1, 0))
        value = 6.0 * offset_view(field, (0, 0, 0)) - beside_all
        bend = second_diff(components[0], target, 0) + second_diff(components[1], target, 1) + second_diff(components[2], target, 2)
        pieces.append(value + (1.0 - penalty) * bend)
    static = jnp.stack(pieces, axis=2)
    current = lam_pad[..., 1:-1, :]
    coupling = omega[:, None, None, None] * sigma[None]
    apply_re = static[:, 0] + coupling[:, None] * current[:, 1]
    apply_im = static[:, 1] - coupling[:, None] * current[:, 0]
    resid_re = (-apply_re).at[:, 0:2, 0].add(surface[:, 0])
    resid_im = (-apply_im).at[:, 0:2, 0].add(surface[:, 1])
    denominator = (diagonal_weight * diagonal_weight + coupling * coupling)[:, None]
    delta_re = (diagonal_weight * resid_re - coupling[:, None] * resid_im) / denominator
    delta_im = (coupling[:, None] * resid_re + diagonal_weight * resid_im) / denominator
    return current + damping * jnp.stack([delta_re, delta_im], axis=1)

def reference(omega, conductivity, forward_field, adjoint_start, station_data, station_owner, station_cell):
    flat_cell = (station_owner[:, 0] * (CX * NY) + station_cell).astype(jnp.int32)
    surface = jnp.zeros((PAIRS, 2, 2, NX * NY), jnp.float32).at[:, :, :, flat_cell].add(station_data)
    surface = surface.reshape(PAIRS, 2, 2, NX, NY)

    def one_pair(carry, inputs):
        frequency, forward, start, source = inputs
        adjoint = start[None]
        for sweep_step in range(SWEEPS):
            widened = jnp.pad(adjoint, ((0, 0), (0, 0), (0, 0), (0, 0), (1, 1), (0, 0)))
            adjoint = relax(widened, conductivity, source[None], frequency[None])
        adjoint = adjoint[0]
        term = frequency * lax.optimization_barrier(jnp.sum(forward[0] * adjoint[1] + forward[1] * adjoint[0], axis=0))
        return (carry + term, adjoint)
    initial = jnp.zeros((NZ, NX, NY), jnp.float32)
    total, adjoint_field = lax.scan(one_pair, initial, (omega, forward_field, adjoint_start, surface))
    gradient = total * (1.0 / math.sqrt(PAIRS))
    return (adjoint_field, gradient)
```

```python
import functools
import math

import jax
import jax.numpy as jnp
from jax import lax
from jax.experimental import pallas as pl
from jax.experimental.pallas import tpu as pltpu
from jax.sharding import PartitionSpec as P

SWEEPS = 4
DAMPING = 0.7
DIAGONAL = 5.0
ROWS = 8
HALF = 4
LEVELS = 16
ALONG = 256
FIELDS = 6
PLANES = FIELDS * LEVELS + LEVELS
PACKED = PLANES // 2


def pack_kernel(field_ref, sigma_ref, first_ref, last_ref):
    low = lax.broadcasted_iota(jnp.int32, (1, ROWS, ALONG), 1) < HALF
    top = FIELDS * LEVELS - PACKED
    upper = field_ref[0:PACKED]
    under = jnp.concatenate([field_ref[PACKED : PACKED + top], sigma_ref[...]], axis=0)
    first_ref[...] = jnp.where(low, upper, pltpu.roll(under, HALF, 1))
    last_ref[...] = jnp.where(low, pltpu.roll(upper, HALF, 1), under)


def surface_kernel(tile_ref, lists_ref, out_ref, acc_ref):
    start = tile_ref[0] * ROWS
    sources = lists_ref.shape[0]
    listed = lists_ref.shape[2]
    row = lax.broadcasted_iota(jnp.int32, (16, listed), 0)
    along = lax.broadcasted_iota(jnp.int32, (ALONG, listed), 0)
    acc_ref[...] = jnp.zeros_like(acc_ref)

    def step(source, carry):
        block = lists_ref[source]
        owner = block[4:5].astype(jnp.int32)
        cell = block[5:6].astype(jnp.int32)
        place = owner * ROWS + (cell >> 8) - start
        inside = (place >= -HALF) & (place < ROWS + HALF)
        place = jnp.where(inside, place & 15, 99)
        here = place == row
        high = block.astype(jnp.bfloat16).astype(jnp.float32)
        rest = block - high
        parts = []
        for which in range(4):
            for value in (high, rest):
                parts.append(
                    jnp.where(here, value[which : which + 1], 0.0).astype(jnp.bfloat16)
                )
        left = jnp.concatenate(parts, axis=0)
        right = jnp.where(along == (cell & 255), 1.0, 0.0).astype(jnp.bfloat16)
        acc_ref[...] += lax.dot_general(
            left, right, (((1,), (1,)), ((), ())), preferred_element_type=jnp.float32
        )
        return carry

    lax.fori_loop(0, sources, step, 0)
    for which in range(4):
        out_ref[which] = acc_ref[32 * which : 32 * which + 16] + acc_ref[32 * which + 16 : 32 * which + 32]


def relax_kernel(
    pairs_all,
    omega_ref,
    tile_ref,
    field_ref,
    forward_hbm,
    sigma_ref,
    below_ref,
    above_ref,
    surface_ref,
    out_ref,
    term_ref,
    one,
    two,
    coef,
    extra,
    grad,
    forward_ref,
    sem,
):
    fetch = pltpu.make_async_copy(forward_hbm, forward_ref, sem)
    fetch.start()
    sub = lax.broadcasted_iota(jnp.int32, (8, 128), 0)
    lane = lax.broadcasted_iota(jnp.int32, (8, 128), 1)
    sub_last, sub_first = sub < 7, sub > 0
    lane_last, lane_first = lane < 127, lane > 0
    low = sub < HALF
    zero = jnp.zeros((8, 128), jnp.float32)
    omega = omega_ref[0]
    tile = tile_ref[0]
    tiles = tile_ref[1]

    def load(ref, *index, rows=2):
        return [
            [ref[(*index, slice(8 * r, 8 * r + 8), slice(128 * c, 128 * c + 128))] for c in range(2)]
            for r in range(rows)
        ]

    def store(ref, value, *index):
        for r, line in enumerate(value):
            for c, piece in enumerate(line):
                ref[(*index, slice(8 * r, 8 * r + 8), slice(128 * c, 128 * c + 128))] = piece

    def both(function, *values):
        rows = min(len(v) for v in values)
        return [[function(*(v[r][c] for v in values)) for c in range(2)] for r in range(rows)]

    def x_next(value, rows=2):
        turned = [[pltpu.roll(value[r][c], 7, 0) for c in range(2)] for r in range(2)]
        return [[jnp.where(sub_last, turned[r][c], turned[1 - r][c]) for c in range(2)] for r in range(rows)]

    def x_prev(value, rows=2):
        turned = [[pltpu.roll(value[r][c], 1, 0) for c in range(2)] for r in range(2)]
        return [[jnp.where(sub_first, turned[r][c], turned[1 - r][c]) for c in range(2)] for r in range(rows)]

    def y_next(value):
        out = []
        for line in value:
            left, right = (pltpu.roll(piece, 127, 1) for piece in line)
            out.append([jnp.where(lane_last, left, right), jnp.where(lane_last, right, zero)])
        return out

    def y_prev(value):
        out = []
        for line in value:
            left, right = (pltpu.roll(piece, 1, 1) for piece in line)
            out.append([jnp.where(lane_first, left, zero), jnp.where(lane_first, right, left)])
        return out

    def plus(a, b):
        return both(lambda p, q: p + q, a, b)

    def minus(a, b):
        return both(lambda p, q: p - q, a, b)

    keep = jnp.where(low, (tile < tiles - 1).astype(jnp.int32), (tile > 0).astype(jnp.int32)) > 0

    def beside(index, upper):
        first, last = above_ref[index], below_ref[index]
        wide = lax.broadcasted_iota(jnp.int32, (8, ALONG), 0) < HALF
        if upper:
            return jnp.where(wide, first, pltpu.roll(last, HALF, 0))
        return jnp.where(wide, pltpu.roll(first, HALF, 0), last)

    blank = jnp.zeros((16, ALONG), jnp.float32)
    for buffer in (one, two):
        for field in range(FIELDS):
            buffer[field, 0] = blank
            buffer[field, LEVELS + 1] = blank
    for part in range(2):
        for edge in (0, LEVELS + 1):
            for kind in range(3):
                grad[kind, part, edge] = blank

    for field in range(FIELDS):

        def fill(level, carry, field=field):
            plane = field * LEVELS + level
            one[field, level + 1, 0:8] = field_ref[plane]
            if field * LEVELS + LEVELS <= PACKED:
                one[field, level + 1, 8:16] = beside(plane, True)
            elif field * LEVELS >= PACKED:
                one[field, level + 1, 8:16] = beside(plane - PACKED, False)
            else:

                @pl.when(plane < PACKED)
                def _():
                    one[field, level + 1, 8:16] = beside(jnp.minimum(plane, PACKED - 1), True)

                @pl.when(plane >= PACKED)
                def _():
                    one[field, level + 1, 8:16] = beside(jnp.maximum(plane - PACKED, 0), False)

            return carry

        lax.fori_loop(0, LEVELS, fill, 0)

    def weights(level, carry):
        inner = sigma_ref[level] * omega
        outer = beside(FIELDS * LEVELS - PACKED + level, False) * omega
        for r, value in enumerate((inner, outer)):
            scale = DAMPING / (DIAGONAL * DIAGONAL + value * value)
            if r == 1:
                wide = jnp.concatenate([keep, keep], axis=1)
                scale = jnp.where(wide, scale, 0.0)
            coef[0, level, 8 * r : 8 * r + 8] = DIAGONAL * scale
            coef[1, level, 8 * r : 8 * r + 8] = value * scale
        return carry

    lax.fori_loop(0, LEVELS, weights, 0)

    for comp in range(2):
        s_re, s_im = surface_ref[comp], surface_ref[2 + comp]
        extra[comp] = coef[0, 0] * s_re - coef[1, 0] * s_im
        extra[2 + comp] = coef[1, 0] * s_re + coef[0, 0] * s_im

    def prepare(source, level):
        for part in range(2):
            u = load(source, 3 * part, level + 1)
            v = load(source, 3 * part + 1, level + 1)
            up, down = x_next(u), x_prev(u)
            gx = minus(up, down)
            nx = plus(up, down)
            up, down = y_next(v), y_prev(v)
            gy = minus(up, down)
            ny = plus(up, down)
            store(grad, gx, 0, part, level + 1)
            store(grad, gy, 1, part, level + 1)
            store(grad, plus(gx, gy), 2, part, level + 1)
            store(grad, nx, 3, part, level + 1)
            store(grad, ny, 4, part, level + 1)

    def combine(own, side, mixed):
        return both(lambda p, q, m: 0.5 * p + q - 0.125 * m, own, side, mixed)

    def finish(source, target, level, last):
        rows = 1 if last else 2
        here = level + 1
        off = []
        for part in range(2):
            base = 3 * part
            u, v, w = (load(source, base + comp, here) for comp in range(3))
            gx, gy = load(grad, 0, part, here), load(grad, 1, part, here)
            wp, wm = load(source, base + 2, here + 1), load(source, base + 2, here - 1)
            gz = minus(wp, wm)
            nzw = plus(wp, wm)
            q = plus(gy, gz)
            mx = minus(x_next(q, rows), x_prev(q, rows))
            q = plus(gx, gz)[:rows]
            my = minus(y_next(q), y_prev(q))
            mz = minus(load(grad, 2, part, here + 1, rows=rows), load(grad, 2, part, here - 1, rows=rows))
            side = plus(y_next(u[:rows]), y_prev(u[:rows]))
            side = plus(side, plus(load(source, base, here + 1, rows=rows), load(source, base, here - 1, rows=rows)))
            cu = combine(load(grad, 3, part, here, rows=rows), side, mx)
            side = plus(x_next(v, rows), x_prev(v, rows))
            side = plus(
                side, plus(load(source, base + 1, here + 1, rows=rows), load(source, base + 1, here - 1, rows=rows))
            )
            cv = combine(load(grad, 4, part, here, rows=rows), side, my)
            side = plus(x_next(w, rows), x_prev(w, rows))
            side = plus(side, plus(y_next(w[:rows]), y_prev(w[:rows])))
            cw = combine(nzw[:rows], side, mz)
            off.append(((u, v, w), (cu, cv, cw)))
        c1, c2 = load(coef, 0, level, rows=rows), load(coef, 1, level, rows=rows)
        results = []
        for comp in range(3):
            re, im = off[0][0][comp][:rows], off[1][0][comp][:rows]
            cr, ci = off[0][1][comp], off[1][1][comp]
            new_re = both(lambda l, a, b, p, q: (1.0 - DAMPING) * l + (a * p - b * q), re, c1, c2, cr, ci)
            new_im = both(lambda l, a, b, p, q: (1.0 - DAMPING) * l + (b * p + a * q), im, c1, c2, cr, ci)
            results.append((new_re, new_im))
            if not last:
                store(target, new_re, comp, here)
                store(target, new_im, 3 + comp, here)
            else:
                store(out_ref, new_re, comp * LEVELS + level)
                store(out_ref, new_im, (3 + comp) * LEVELS + level)

    buffers = (one, two)
    for sweep in range(SWEEPS):
        source, target = buffers[sweep % 2], buffers[1 - sweep % 2]
        last = sweep == SWEEPS - 1
        prepare(source, 0)

        def plane(level, carry, source=source, target=target, last=last):
            prepare(source, level + 1)
            finish(source, target, level, last)
            return carry

        lax.fori_loop(0, LEVELS - 1, plane, 0)
        finish(source, target, LEVELS - 1, last)
        for part in range(2):
            for comp in range(2):
                if last:
                    index = (3 * part + comp) * LEVELS
                    out_ref[index] += extra[2 * part + comp, 0:8]
                else:
                    target[3 * part + comp, 1] += extra[2 * part + comp]

    fetch.wait()
    scale = omega * (1.0 / math.sqrt(pairs_all))

    def gather(level, carry):
        total = jnp.zeros((8, ALONG), jnp.float32)
        for comp in range(3):
            re, im = comp * LEVELS + level, (3 + comp) * LEVELS + level
            total = total + (forward_ref[re] * out_ref[im] + forward_ref[im] * out_ref[re])
        term_ref[level] = total * scale
        return carry

    lax.fori_loop(0, LEVELS, gather, 0)


def body(
    omega, conductivity, forward_field, adjoint_start, station_data, station_owner, station_cell
):
    listed = station_cell.shape[0]
    tiles = lax.axis_size("tile")
    groups = lax.axis_size("freq")
    me = lax.axis_index("tile")
    tile = jnp.stack([me, jnp.int32(tiles)]).astype(jnp.int32)
    field = adjoint_start.reshape(FIELDS * LEVELS, ROWS, ALONG)
    forward = forward_field.reshape(FIELDS * LEVELS, ROWS, ALONG)

    vmem = pl.BlockSpec(memory_space=pltpu.VMEM)
    smem = pl.BlockSpec(memory_space=pltpu.SMEM)
    f32 = jnp.float32

    lists = jnp.concatenate(
        [
            station_data.reshape(4, listed),
            station_owner.reshape(1, listed).astype(f32),
            station_cell.reshape(1, listed).astype(f32),
            jnp.zeros((2, listed), f32),
        ],
        axis=0,
    )
    sent = jnp.broadcast_to(lists[None], (tiles, 8, listed))
    got = lax.all_to_all(sent, "tile", 0, 0, tiled=True)

    first, last = pl.pallas_call(
        pack_kernel,
        out_shape=(
            jax.ShapeDtypeStruct((PACKED, ROWS, ALONG), f32),
            jax.ShapeDtypeStruct((PACKED, ROWS, ALONG), f32),
        ),
        in_specs=[vmem, vmem],
        out_specs=(vmem, vmem),
        compiler_params=pltpu.CompilerParams(vmem_limit_bytes=8 << 20),
        name="pack",
    )(field, conductivity)
    onward = [(i, i + 1) for i in range(tiles - 1)]
    back = [(i + 1, i) for i in range(tiles - 1)]
    below = lax.ppermute(last, "tile", onward)
    above = lax.ppermute(first, "tile", back)

    surface = pl.pallas_call(
        surface_kernel,
        out_shape=jax.ShapeDtypeStruct((4, 16, ALONG), f32),
        in_specs=[smem, vmem],
        out_specs=vmem,
        scratch_shapes=[pltpu.VMEM((128, ALONG), f32)],
        compiler_params=pltpu.CompilerParams(vmem_limit_bytes=8 << 20),
        name="surface",
    )(tile, got)

    adjoint, term = pl.pallas_call(
        functools.partial(relax_kernel, groups),
        out_shape=(
            jax.ShapeDtypeStruct((FIELDS * LEVELS, ROWS, ALONG), f32),
            jax.ShapeDtypeStruct((LEVELS, ROWS, ALONG), f32),
        ),
        in_specs=[smem, smem, vmem, pl.BlockSpec(memory_space=pl.ANY), vmem, vmem, vmem, vmem],
        out_specs=(vmem, vmem),
        scratch_shapes=[
            pltpu.VMEM((FIELDS, LEVELS + 2, 16, ALONG), f32),
            pltpu.VMEM((FIELDS, LEVELS + 2, 16, ALONG), f32),
            pltpu.VMEM((2, LEVELS, 16, ALONG), f32),
            pltpu.VMEM((4, 16, ALONG), f32),
            pltpu.VMEM((5, 2, LEVELS + 2, 16, ALONG), f32),
            pltpu.VMEM((FIELDS * LEVELS, ROWS, ALONG), f32),
            pltpu.SemaphoreType.DMA,
        ],
        compiler_params=pltpu.CompilerParams(vmem_limit_bytes=32 << 20),
        name="relax",
    )(omega, tile, field, forward, conductivity, below, above, surface)

    terms = lax.all_to_all(term, "freq", 0, 0, tiled=True)
    gradient = terms.reshape(groups, LEVELS // groups, ROWS, ALONG).sum(axis=0)
    return (adjoint.reshape(adjoint_start.shape), gradient)


def solution(mesh):
    return jax.shard_map(
        body,
        mesh=mesh,
        in_specs=(
            P("freq"),
            P(None, "tile", None),
            P("freq", None, None, None, "tile", None),
            P("freq", None, None, None, "tile", None),
            P("freq", None, None, "tile"),
            P("tile", None),
            P("tile"),
        ),
        out_specs=(P("freq", None, None, None, "tile", None), P("freq", "tile", None)),
        check_vma=False,
    )
```

```python
import functools
import math

import jax
import jax.numpy as jnp
from jax import lax
from jax.experimental import pallas as pl
from jax.experimental.pallas import tpu as pltpu
from jax.sharding import PartitionSpec as P

SWEEPS = 4
DAMPING = 0.7
DIAGONAL = 5.0
ROWS = 8
HALF = 4
WIDE = 16
LEVELS = 16
ALONG = 256
FIELDS = 6
KINDS = FIELDS + 1
LINES = FIELDS * LEVELS * WIDE
HALO = HALF * KINDS * 2 * LEVELS
f32 = jnp.float32


def as_lines(planes):
    return planes.reshape(-1, ROWS, 2, 128).transpose(0, 2, 1, 3).reshape(-1, 128)


def from_lines(lines):
    return lines.reshape(-1, 2, ROWS, 128).transpose(0, 2, 1, 3).reshape(-1, ROWS, ALONG)


def pack_kernel(field_hbm, sigma_hbm, first_hbm, last_hbm, field_ref, sigma_ref, first_ref, last_ref, in_sems, out_sems):
    size = LEVELS * WIDE
    block = HALF * 2 * LEVELS
    pairs = [
        (field_hbm.at[pl.ds(kind * size, size)], field_ref.at[pl.ds(kind * size, size)])
        for kind in range(FIELDS)
    ]
    pairs.append((sigma_hbm, sigma_ref))
    copies = [
        pltpu.make_async_copy(source, target, in_sems.at[which]) for which, (source, target) in enumerate(pairs)
    ]
    for copy in copies:
        copy.start()
    sends = []
    for kind in range(KINDS):
        copies[kind].wait()
        source, base = (field_ref, kind * LEVELS) if kind < FIELDS else (sigma_ref, 0)
        for x in range(ROWS):
            target = first_ref if x < HALF else last_ref
            for side in range(2):
                for part in range(2):
                    start = (base + 8 * part) * WIDE + side * 8 + x
                    place = ((kind * HALF + x % HALF) * 2 + side) * LEVELS + 8 * part
                    target[place : place + 8] = source[pl.ds(start, 8, stride=WIDE), :]
        rows = pl.ds(kind * block, block)
        for which, (source, target) in enumerate(((first_ref, first_hbm), (last_ref, last_hbm))):
            copy = pltpu.make_async_copy(source.at[rows], target.at[rows], out_sems.at[2 * kind + which])
            copy.start()
            sends.append(copy)
    for copy in sends:
        copy.wait()


def lists_kernel(data_hbm, owner_hbm, cell_hbm, sent_hbm, data_ref, owner_ref, cell_ref, block_ref, in_sems, out_sems):
    copies = [
        pltpu.make_async_copy(source, target, in_sems.at[which])
        for which, (source, target) in enumerate(
            ((data_hbm, data_ref), (owner_hbm, owner_ref), (cell_hbm, cell_ref))
        )
    ]
    for copy in copies:
        copy.start()
    for copy in copies:
        copy.wait()
    for chunk in range(block_ref.shape[0] // 6):
        lanes = slice(128 * chunk, 128 * chunk + 128)
        row = 6 * chunk
        block_ref[row : row + 2] = data_ref[0, :, lanes]
        block_ref[row + 2 : row + 4] = data_ref[1, :, lanes]
        block_ref[row + 4 : row + 5] = owner_ref[:, lanes].astype(f32)
        block_ref[row + 5 : row + 6] = cell_ref[:, lanes].astype(f32)
    sends = [
        pltpu.make_async_copy(block_ref, sent_hbm.at[tile], out_sems.at[tile]) for tile in range(sent_hbm.shape[0])
    ]
    for copy in sends:
        copy.start()
    for copy in sends:
        copy.wait()


def surface_kernel(place_ref, lists_ref, out_ref, acc_ref):
    start = place_ref[0] * ROWS - HALF
    sources = lists_ref.shape[0]
    chunks = lists_ref.shape[1] // 6
    row = lax.broadcasted_iota(jnp.int32, (WIDE, 128), 0)
    along = lax.broadcasted_iota(jnp.int32, (ALONG, 128), 0)
    acc_ref[...] = jnp.zeros_like(acc_ref)

    def step(source, carry):
        lefts, rights = [], []
        for chunk in range(chunks):
            block = lists_ref[source, 6 * chunk : 6 * chunk + 6]
            owner = block[4:5].astype(jnp.int32)
            cell = block[5:6].astype(jnp.int32)
            here = owner * ROWS + (cell >> 8) - start == row
            high = block[0:4].astype(jnp.bfloat16).astype(f32)
            rest = block[0:4] - high
            parts = []
            for which in range(4):
                for value in (high, rest):
                    parts.append(jnp.where(here, value[which : which + 1], 0.0).astype(jnp.bfloat16))
            lefts.append(jnp.concatenate(parts, axis=0))
            rights.append(jnp.where(along == (cell & 255), 1.0, 0.0).astype(jnp.bfloat16))
        acc_ref[...] += lax.dot_general(
            jnp.concatenate(lefts, axis=1),
            jnp.concatenate(rights, axis=1),
            (((1,), (1,)), ((), ())),
            preferred_element_type=f32,
        )
        return carry

    lax.fori_loop(0, sources, step, 0)
    top = lax.broadcasted_iota(jnp.int32, (8, 128), 0) == 0
    for which in range(4):
        total = acc_ref[32 * which : 32 * which + 16] + acc_ref[32 * which + 16 : 32 * which + 32]
        for x in range(WIDE):
            for side in range(2):
                line = total[x : x + 1, 128 * side : 128 * side + 128]
                out_ref[which, x, side] = jnp.where(top, line, 0.0)


def quarters(place_ref, below_ref, above_ref):
    tile, tiles = place_ref[0], place_ref[1]
    return ((0, below_ref, tile > 0), (HALF + ROWS, above_ref, tile < tiles - 1))


def packed(ref, x, kind, side, part):
    start = ((kind * HALF + x) * 2 + side) * LEVELS + 8 * part
    return ref[pl.ds(pl.multiple_of(start, 8), 8), :]


def coef_kernel(omega_ref, place_ref, below_ref, sigma_ref, above_ref, coef):
    omega = omega_ref[0]

    def store(value, at, side, part, inside):
        value = value * omega
        scale = DAMPING / (DIAGONAL * DIAGONAL + value * value)
        if inside is not None:
            scale = jnp.where(inside, scale, 0.0)
        coef[0, at, side, 8 * part : 8 * part + 8] = DIAGONAL * scale
        coef[1, at, side, 8 * part : 8 * part + 8] = value * scale

    for base, ref, inside in quarters(place_ref, below_ref, above_ref):
        for x in range(HALF):
            for side in range(2):
                for part in range(2):
                    store(packed(ref, x, FIELDS, side, part), base + x, side, part, inside)
    for x in range(ROWS):
        for side in range(2):
            for part in range(2):
                value = sigma_ref[pl.ds(8 * part * WIDE + side * 8 + x, 8, stride=WIDE), :]
                store(value, HALF + x, side, part, None)


def relax_kernel(
    pairs_all,
    omega_ref,
    place_ref,
    below_ref,
    field_ref,
    above_ref,
    coef,
    surface_ref,
    forward_ref,
    out_ref,
    term_ref,
    one,
    two,
    total_ref,
):
    lane = lax.broadcasted_iota(jnp.int32, (8, 128), 1)
    lane_last, lane_first = lane < 127, lane > 0
    zero = jnp.zeros((8, 128), f32)
    omega = omega_ref[0]

    def clear(x, carry):
        for side in range(2):
            for field in range(FIELDS):
                for buffer in (one, two):
                    buffer[field, x, side, 0:8] = zero
                    buffer[field, x, side, 24:32] = zero
        return carry

    lax.fori_loop(0, WIDE, clear, 0)

    for base, ref, inside in quarters(place_ref, below_ref, above_ref):

        def outer(x, carry, base=base, ref=ref, inside=inside):
            for side in range(2):
                for part in range(2):
                    for field in range(FIELDS):
                        value = jnp.where(inside, packed(ref, x, field, side, part), 0.0)
                        one[field, base + x, side, 8 + 8 * part : 16 + 8 * part] = value
            return carry

        lax.fori_loop(0, HALF, outer, 0)

    def inner(x, carry):
        for side in range(2):
            for part in range(2):
                for field in range(FIELDS):
                    start = (field * LEVELS + 8 * part) * WIDE + side * 8 + x
                    value = field_ref[pl.ds(start, 8, stride=WIDE), :]
                    one[field, HALF + x, side, 8 + 8 * part : 16 + 8 * part] = value
        return carry

    lax.fori_loop(0, ROWS, inner, 0)

    def y_sum(ahead, behind):
        left, right = (pltpu.roll(piece, 127, 1) for piece in ahead)
        low, high = (pltpu.roll(piece, 1, 1) for piece in behind)
        return [
            jnp.where(lane_last, left, right) + jnp.where(lane_first, low, zero),
            jnp.where(lane_last, right, zero) + jnp.where(lane_first, high, low),
        ]

    def advance(x, source, target, last):
        for part in range(2):
            row = 8 + 8 * part
            off, old = [], []
            for half in range(2):
                ahead, behind, rest = ([], [], []), ([], [], []), ([], [], [])
                for side in range(2):

                    def at(comp, dx=0, dz=0, side=side, half=half):
                        return source[3 * half + comp, x + dx, side, row + dz : row + dz + 8]

                    u, v, w = at(0), at(1), at(2)
                    old.append((u, v, w))
                    up, down = at(0, 1), at(0, -1)
                    dxu, nxu = up - down, up + down
                    up, down = at(1, 1), at(1, -1)
                    dxv, nxv = up - down, up + down
                    up, down = at(1, 0, 1), at(1, 0, -1)
                    dzv, nzv = up - down, up + down
                    up, down = at(2, 0, 1), at(2, 0, -1)
                    dzw, nzw = up - down, up + down
                    nxw = at(2, 1) + at(2, -1)
                    nzu = at(0, 0, 1) + at(0, 0, -1)
                    ddw = (at(2, 1, 1) - at(2, 1, -1)) - (at(2, -1, 1) - at(2, -1, -1))
                    ddu = (at(0, 1, 1) - at(0, 1, -1)) - (at(0, -1, 1) - at(0, -1, -1))
                    for comp, (middle, slope) in enumerate(
                        ((u, 0.125 * dxv), (0.5 * v, 0.125 * (dxu + dzw)), (w, 0.125 * dzv))
                    ):
                        ahead[comp].append(middle - slope)
                        behind[comp].append(middle + slope)
                    rest[0].append((0.5 * nxu + nzu) - 0.125 * ddw)
                    rest[1].append(nxv + nzv)
                    rest[2].append((0.5 * nzw + nxw) - 0.125 * ddu)
                for comp in range(3):
                    sums = y_sum(ahead[comp], behind[comp])
                    value = [rest[comp][side] + sums[side] for side in range(2)]
                    if part == 0 and comp < 2:
                        value = [value[side] + surface_ref[2 * half + comp, x, side] for side in range(2)]
                    off.append(value)
            for side in range(2):
                c1 = coef[0, x, side, 8 * part : 8 * part + 8]
                c2 = coef[1, x, side, 8 * part : 8 * part + 8]
                total = None
                for comp in range(3):
                    re, im = off[comp][side], off[3 + comp][side]
                    new_re = (1.0 - DAMPING) * old[side][comp] + (c1 * re - c2 * im)
                    new_im = (1.0 - DAMPING) * old[2 + side][comp] + (c2 * re + c1 * im)
                    if not last:
                        target[comp, x, side, row : row + 8] = new_re
                        target[3 + comp, x, side, row : row + 8] = new_im
                    else:
                        base = side * 8 + x - HALF
                        re_at = pl.ds((comp * LEVELS + 8 * part) * WIDE + base, 8, stride=WIDE)
                        im_at = pl.ds(((3 + comp) * LEVELS + 8 * part) * WIDE + base, 8, stride=WIDE)
                        out_ref[re_at, :] = new_re
                        out_ref[im_at, :] = new_im
                        piece = forward_ref[re_at, :] * new_im + forward_ref[im_at, :] * new_re
                        total = piece if total is None else total + piece
                if last:
                    total_ref[pl.ds(8 * part * WIDE + side * 8 + x - HALF, 8, stride=WIDE), :] = total

    buffers = (one, two)
    for sweep in range(SWEEPS):
        source, target = buffers[sweep % 2], buffers[1 - sweep % 2]
        last = sweep == SWEEPS - 1

        def slice_of(step, carry, source=source, target=target, last=last, begin=1 + sweep):
            for x in range(2):
                advance(begin + 2 * step + x, source, target, last)
            return carry

        lax.fori_loop(0, (WIDE - 2 - 2 * sweep) // 2, slice_of, 0)

    scale = omega * (1.0 / math.sqrt(pairs_all))
    term_ref[...] = total_ref[...] * scale


def body(
    omega, conductivity, forward_field, adjoint_start, station_data, station_owner, station_cell
):
    listed = station_cell.shape[0]
    tiles = lax.axis_size("tile")
    groups = lax.axis_size("freq")
    place = jnp.stack([lax.axis_index("tile"), jnp.int32(tiles)])

    vmem = pl.BlockSpec(memory_space=pltpu.VMEM)
    smem = pl.BlockSpec(memory_space=pltpu.SMEM)

    far = pl.BlockSpec(memory_space=pltpu.HBM)
    sent = pl.pallas_call(
        lists_kernel,
        out_shape=jax.ShapeDtypeStruct((tiles, 6 * listed // 128, 128), f32),
        in_specs=[far] * 3,
        out_specs=far,
        scratch_shapes=[
            pltpu.VMEM((2, 2, listed), f32),
            pltpu.VMEM((1, listed), jnp.int32),
            pltpu.VMEM((1, listed), jnp.int32),
            pltpu.VMEM((6 * listed // 128, 128), f32),
            pltpu.SemaphoreType.DMA((3,)),
            pltpu.SemaphoreType.DMA((tiles,)),
        ],
        name="lists",
    )(station_data.reshape(2, 2, listed), station_owner.reshape(1, listed), station_cell.reshape(1, listed))
    first, last = pl.pallas_call(
        pack_kernel,
        out_shape=(
            jax.ShapeDtypeStruct((HALO, 128), f32),
            jax.ShapeDtypeStruct((HALO, 128), f32),
        ),
        in_specs=[far] * 2,
        out_specs=(far, far),
        scratch_shapes=[
            pltpu.VMEM((LINES, 128), f32),
            pltpu.VMEM((LEVELS * WIDE, 128), f32),
            pltpu.VMEM((HALO, 128), f32),
            pltpu.VMEM((HALO, 128), f32),
            pltpu.SemaphoreType.DMA((KINDS,)),
            pltpu.SemaphoreType.DMA((2 * KINDS,)),
        ],
        name="pack",
    )(as_lines(adjoint_start), as_lines(conductivity))
    below = lax.ppermute(last, "tile", [(i, (i + 1) % tiles) for i in range(tiles)])
    above = lax.ppermute(first, "tile", [((i + 1) % tiles, i) for i in range(tiles)])
    got = lax.all_to_all(sent, "tile", 0, 0, tiled=True)

    surface = pl.pallas_call(
        surface_kernel,
        out_shape=jax.ShapeDtypeStruct((4, WIDE, 2, 8, 128), f32),
        in_specs=[smem, vmem],
        out_specs=vmem,
        scratch_shapes=[pltpu.VMEM((128, ALONG), f32)],
        compiler_params=pltpu.CompilerParams(vmem_limit_bytes=4 << 20),
        cost_estimate=pl.CostEstimate(flops=10**9, bytes_accessed=10**6, transcendentals=0),
        name="surface",
    )(place, got)

    coef = pl.pallas_call(
        coef_kernel,
        out_shape=jax.ShapeDtypeStruct((2, WIDE, 2, LEVELS, 128), f32),
        in_specs=[smem, smem] + [vmem] * 3,
        out_specs=vmem,
        compiler_params=pltpu.CompilerParams(vmem_limit_bytes=4 << 20),
        name="coef",
    )(omega, place, below, as_lines(conductivity), above)

    adjoint, term = pl.pallas_call(
        functools.partial(relax_kernel, groups),
        out_shape=(
            jax.ShapeDtypeStruct((LINES, 128), f32),
            jax.ShapeDtypeStruct((LEVELS * WIDE, 128), f32),
        ),
        in_specs=[smem, smem] + [vmem] * 6,
        out_specs=(vmem, vmem),
        scratch_shapes=[
            pltpu.VMEM((FIELDS, WIDE, 2, 32, 128), f32),
            pltpu.VMEM((FIELDS, WIDE, 2, 32, 128), f32),
            pltpu.VMEM((LEVELS * WIDE, 128), f32),
        ],
        compiler_params=pltpu.CompilerParams(vmem_limit_bytes=12 << 20),
        name="relax",
    )(omega, place, below, as_lines(adjoint_start), above, coef, surface, as_lines(forward_field))

    terms = lax.all_to_all(term.reshape(groups, -1, 128), "freq", 0, 0, tiled=True)
    gradient = from_lines(terms.sum(axis=0))
    return (from_lines(adjoint).reshape(adjoint_start.shape), gradient)


def solution(mesh):
    return jax.shard_map(
        body,
        mesh=mesh,
        in_specs=(
            P("freq"),
            P(None, "tile", None),
            P("freq", None, None, None, "tile", None),
            P("freq", None, None, None, "tile", None),
            P("freq", None, None, "tile"),
            P("tile", None),
            P("tile"),
        ),
        out_specs=(P("freq", None, None, None, "tile", None), P("freq", "tile", None)),
        check_vma=False,
    )
```

```python
import functools
import math

import jax
import jax.numpy as jnp
from jax import lax
from jax.experimental import pallas as pl
from jax.experimental.pallas import tpu as pltpu
from jax.sharding import PartitionSpec as P

SWEEPS = 4
DAMPING = 0.7
DIAGONAL = 5.0
ROWS = 8
HALF = 4
WIDE = 16
LEVELS = 16
ALONG = 256
FIELDS = 6
KINDS = FIELDS + 1
LINES = FIELDS * LEVELS * WIDE
HALO = HALF * KINDS * 2 * LEVELS
f32 = jnp.float32


def as_lines(planes):
    return planes.reshape(-1, ROWS, 2, 128).transpose(0, 2, 1, 3).reshape(-1, 128)


def from_lines(lines):
    return lines.reshape(-1, 2, ROWS, 128).transpose(0, 2, 1, 3).reshape(-1, ROWS, ALONG)


def pack_kernel(field_ref, sigma_ref, first_ref, last_ref):
    for kind in range(KINDS):
        source, base = (field_ref, kind * LEVELS) if kind < FIELDS else (sigma_ref, 0)
        for x in range(ROWS):
            target = first_ref if x < HALF else last_ref
            for side in range(2):
                for part in range(2):
                    start = (base + 8 * part) * WIDE + side * 8 + x
                    place = ((kind * HALF + x % HALF) * 2 + side) * LEVELS + 8 * part
                    target[place : place + 8] = source[pl.ds(start, 8, stride=WIDE), :]


def lists_kernel(data_hbm, owner_hbm, cell_hbm, sent_hbm, data_ref, owner_ref, cell_ref, block_ref, in_sems, out_sems):
    copies = [
        pltpu.make_async_copy(source, target, in_sems.at[which])
        for which, (source, target) in enumerate(
            ((data_hbm, data_ref), (owner_hbm, owner_ref), (cell_hbm, cell_ref))
        )
    ]
    for copy in copies:
        copy.start()
    for copy in copies:
        copy.wait()
    for chunk in range(block_ref.shape[0] // 6):
        lanes = slice(128 * chunk, 128 * chunk + 128)
        row = 6 * chunk
        block_ref[row : row + 2] = data_ref[0, :, lanes]
        block_ref[row + 2 : row + 4] = data_ref[1, :, lanes]
        block_ref[row + 4 : row + 5] = owner_ref[:, lanes].astype(f32)
        block_ref[row + 5 : row + 6] = cell_ref[:, lanes].astype(f32)
    sends = [
        pltpu.make_async_copy(block_ref, sent_hbm.at[tile], out_sems.at[tile]) for tile in range(sent_hbm.shape[0])
    ]
    for copy in sends:
        copy.start()
    for copy in sends:
        copy.wait()


def store_kernel(value_ref, out_hbm, sems):
    count = sems.shape[0]
    size = value_ref.shape[0] // count
    copies = [
        pltpu.make_async_copy(
            value_ref.at[pl.ds(size * which, size)], out_hbm.at[pl.ds(size * which, size)], sems.at[which]
        )
        for which in range(count)
    ]
    for copy in copies:
        copy.start()
    for copy in copies:
        copy.wait()


def quarters(place_ref, below_ref, above_ref):
    tile, tiles = place_ref[0], place_ref[1]
    return ((0, below_ref, tile > 0), (HALF + ROWS, above_ref, tile < tiles - 1))


def packed(ref, x, kind, side, part):
    start = ((kind * HALF + x) * 2 + side) * LEVELS + 8 * part
    return ref[pl.ds(pl.multiple_of(start, 8), 8), :]


def set_weights(coef, omega, value, at, side, part, inside=None):
    value = value * omega
    scale = DAMPING / (DIAGONAL * DIAGONAL + value * value)
    if inside is not None:
        scale = jnp.where(inside, scale, 0.0)
    coef[0, at, side, 8 * part : 8 * part + 8] = DIAGONAL * scale
    coef[1, at, side, 8 * part : 8 * part + 8] = value * scale


def y_sum(ahead, behind):
    lane = lax.broadcasted_iota(jnp.int32, (8, 128), 1)
    lane_last, lane_first = lane < 127, lane > 0
    left, right = (pltpu.roll(piece, 127, 1) for piece in ahead)
    low, high = (pltpu.roll(piece, 1, 1) for piece in behind)
    return [
        jnp.where(lane_last, left, right) + jnp.where(lane_first, low, 0.0),
        jnp.where(lane_last, right, 0.0) + jnp.where(lane_first, high, low),
    ]


def advance(x, source, coef, surface_ref, emit):
    for part in range(2):
        row = 8 + 8 * part
        off, old = [], []
        for half in range(2):
            ahead, behind, rest = ([], [], []), ([], [], []), ([], [], [])
            for side in range(2):

                def at(comp, dx=0, dz=0, side=side, half=half):
                    return source[3 * half + comp, x + dx, side, row + dz : row + dz + 8]

                u, v, w = at(0), at(1), at(2)
                old.append((u, v, w))
                up, down = at(0, 1), at(0, -1)
                dxu, nxu = up - down, up + down
                up, down = at(1, 1), at(1, -1)
                dxv, nxv = up - down, up + down
                up, down = at(1, 0, 1), at(1, 0, -1)
                dzv, nzv = up - down, up + down
                up, down = at(2, 0, 1), at(2, 0, -1)
                dzw, nzw = up - down, up + down
                nxw = at(2, 1) + at(2, -1)
                nzu = at(0, 0, 1) + at(0, 0, -1)
                ddw = (at(2, 1, 1) - at(2, 1, -1)) - (at(2, -1, 1) - at(2, -1, -1))
                ddu = (at(0, 1, 1) - at(0, 1, -1)) - (at(0, -1, 1) - at(0, -1, -1))
                for comp, (middle, slope) in enumerate(
                    ((u, 0.125 * dxv), (0.5 * v, 0.125 * (dxu + dzw)), (w, 0.125 * dzv))
                ):
                    ahead[comp].append(middle - slope)
                    behind[comp].append(middle + slope)
                rest[0].append((0.5 * nxu + nzu) - 0.125 * ddw)
                rest[1].append(nxv + nzv)
                rest[2].append((0.5 * nzw + nxw) - 0.125 * ddu)
            for comp in range(3):
                sums = y_sum(ahead[comp], behind[comp])
                value = [rest[comp][side] + sums[side] for side in range(2)]
                if part == 0 and comp < 2:
                    value = [value[side] + surface_ref[2 * half + comp, x, side] for side in range(2)]
                off.append(value)
        for side in range(2):
            c1 = coef[0, x, side, 8 * part : 8 * part + 8]
            c2 = coef[1, x, side, 8 * part : 8 * part + 8]
            news = []
            for comp in range(3):
                re, im = off[comp][side], off[3 + comp][side]
                new_re = (1.0 - DAMPING) * old[side][comp] + (c1 * re - c2 * im)
                new_im = (1.0 - DAMPING) * old[2 + side][comp] + (c2 * re + c1 * im)
                news.append((new_re, new_im))
            emit(x, side, part, news)


def keep_in(target):
    def emit(x, side, part, news):
        for comp, (new_re, new_im) in enumerate(news):
            target[comp, x, side, 8 + 8 * part : 16 + 8 * part] = new_re
            target[3 + comp, x, side, 8 + 8 * part : 16 + 8 * part] = new_im

    return emit


def surface_kernel(place_ref, lists_ref, out_ref, acc_ref):
    start = place_ref[0] * ROWS - HALF
    sources = lists_ref.shape[0]
    chunks = lists_ref.shape[1] // 6
    row = lax.broadcasted_iota(jnp.int32, (WIDE, 128), 0)
    along = lax.broadcasted_iota(jnp.int32, (ALONG, 128), 0)
    acc_ref[...] = jnp.zeros_like(acc_ref)

    def step(source, carry):
        lefts, rights = [], []
        for chunk in range(chunks):
            block = lists_ref[source, 6 * chunk : 6 * chunk + 6]
            owner = block[4:5].astype(jnp.int32)
            cell = block[5:6].astype(jnp.int32)
            here = owner * ROWS + (cell >> 8) - start == row
            high = block[0:4].astype(jnp.bfloat16).astype(f32)
            rest = block[0:4] - high
            parts = []
            for which in range(4):
                for value in (high, rest):
                    parts.append(jnp.where(here, value[which : which + 1], 0.0).astype(jnp.bfloat16))
            lefts.append(jnp.concatenate(parts, axis=0))
            rights.append(jnp.where(along == (cell & 255), 1.0, 0.0).astype(jnp.bfloat16))
        acc_ref[...] += lax.dot_general(
            jnp.concatenate(lefts, axis=1),
            jnp.concatenate(rights, axis=1),
            (((1,), (1,)), ((), ())),
            preferred_element_type=f32,
        )
        return carry

    lax.fori_loop(0, sources, step, 0)
    top = lax.broadcasted_iota(jnp.int32, (8, 128), 0) == 0
    for which in range(4):
        total = acc_ref[32 * which : 32 * which + 16] + acc_ref[32 * which + 16 : 32 * which + 32]
        for x in range(WIDE):
            for side in range(2):
                line = total[x : x + 1, 128 * side : 128 * side + 128]
                out_ref[which, x, side] = jnp.where(top, line, 0.0)


def inner_kernel(omega_ref, field_ref, sigma_ref, surface_ref, one, two, coef):
    omega = omega_ref[0]
    zero = jnp.zeros((8, 128), f32)

    def clear(x, carry):
        for side in range(2):
            for field in range(FIELDS):
                for buffer in (one, two):
                    buffer[field, x, side, 0:8] = zero
                    buffer[field, x, side, 24:32] = zero
        return carry

    lax.fori_loop(0, WIDE, clear, 0)

    def fill(x, carry):
        for side in range(2):
            for part in range(2):
                for field in range(FIELDS):
                    at = (field * LEVELS + 8 * part) * WIDE + side * 8 + x
                    value = field_ref[pl.ds(at, 8, stride=WIDE), :]
                    one[field, HALF + x, side, 8 + 8 * part : 16 + 8 * part] = value
                value = sigma_ref[pl.ds(8 * part * WIDE + side * 8 + x, 8, stride=WIDE), :]
                set_weights(coef, omega, value, HALF + x, side, part)
        return carry

    lax.fori_loop(0, ROWS, fill, 0)

    buffers = (one, two)
    for sweep in range(SWEEPS - 1):
        source, target = buffers[sweep % 2], buffers[1 - sweep % 2]

        def slices(step, carry, source=source, target=target, begin=HALF + 1 + sweep):
            for x in range(2):
                advance(begin + 2 * step + x, source, coef, surface_ref, keep_in(target))
            return carry

        lax.fori_loop(0, ROWS // 2 - 1 - sweep, slices, 0)


def outer_kernel(
    pairs_all,
    omega_ref,
    place_ref,
    below_ref,
    above_ref,
    one_in,
    two_in,
    coef_in,
    surface_ref,
    forward_ref,
    out_ref,
    term_ref,
    one,
    two,
    coef,
):
    omega = omega_ref[0]
    scale = omega * (1.0 / math.sqrt(pairs_all))

    for base, ref, inside in quarters(place_ref, below_ref, above_ref):

        def fill(x, carry, base=base, ref=ref, inside=inside):
            for side in range(2):
                for part in range(2):
                    for field in range(FIELDS):
                        value = jnp.where(inside, packed(ref, x, field, side, part), 0.0)
                        one[field, base + x, side, 8 + 8 * part : 16 + 8 * part] = value
                    value = packed(ref, x, FIELDS, side, part)
                    set_weights(coef, omega, value, base + x, side, part, inside)
            return carry

        lax.fori_loop(0, HALF, fill, 0)

    def give_out(x, side, part, news):
        base = side * 8 + x - HALF
        total = None
        for comp, (new_re, new_im) in enumerate(news):
            re_at = pl.ds((comp * LEVELS + 8 * part) * WIDE + base, 8, stride=WIDE)
            im_at = pl.ds(((3 + comp) * LEVELS + 8 * part) * WIDE + base, 8, stride=WIDE)
            out_ref[re_at, :] = new_re
            out_ref[im_at, :] = new_im
            piece = forward_ref[re_at, :] * new_im + forward_ref[im_at, :] * new_re
            total = piece if total is None else total + piece
        term_ref[pl.ds(8 * part * WIDE + base, 8, stride=WIDE), :] = total * scale

    buffers = (one, two)
    for sweep in range(SWEEPS):
        source, target = buffers[sweep % 2], buffers[1 - sweep % 2]
        emit = give_out if sweep == SWEEPS - 1 else keep_in(target)

        def slices(step, carry, source=source, emit=emit, sweep=sweep):
            for x in range(2):
                advance(1 + sweep + 2 * step + x, source, coef, surface_ref, emit)
                advance(WIDE - 1 - HALF - sweep + 2 * step + x, source, coef, surface_ref, emit)
            return carry

        lax.fori_loop(0, HALF // 2, slices, 0)


def body(
    omega, conductivity, forward_field, adjoint_start, station_data, station_owner, station_cell
):
    listed = station_cell.shape[0]
    tiles = lax.axis_size("tile")
    groups = lax.axis_size("freq")
    place = jnp.stack([lax.axis_index("tile"), jnp.int32(tiles)])

    vmem = pl.BlockSpec(memory_space=pltpu.VMEM)
    smem = pl.BlockSpec(memory_space=pltpu.SMEM)

    far = pl.BlockSpec(memory_space=pltpu.HBM)
    sent = pl.pallas_call(
        lists_kernel,
        out_shape=jax.ShapeDtypeStruct((tiles, 6 * listed // 128, 128), f32),
        in_specs=[far] * 3,
        out_specs=far,
        scratch_shapes=[
            pltpu.VMEM((2, 2, listed), f32),
            pltpu.VMEM((1, listed), jnp.int32),
            pltpu.VMEM((1, listed), jnp.int32),
            pltpu.VMEM((6 * listed // 128, 128), f32),
            pltpu.SemaphoreType.DMA((3,)),
            pltpu.SemaphoreType.DMA((tiles,)),
        ],
        cost_estimate=pl.CostEstimate(flops=10**9, bytes_accessed=10**6, transcendentals=0),
        name="lists",
    )(station_data.reshape(2, 2, listed), station_owner.reshape(1, listed), station_cell.reshape(1, listed))
    first, last = pl.pallas_call(
        pack_kernel,
        out_shape=(jax.ShapeDtypeStruct((HALO, 128), f32), jax.ShapeDtypeStruct((HALO, 128), f32)),
        in_specs=[vmem] * 2,
        out_specs=(vmem, vmem),
        compiler_params=pltpu.CompilerParams(vmem_limit_bytes=1 << 20),
        name="pack",
    )(as_lines(adjoint_start), as_lines(conductivity))
    below = lax.ppermute(last, "tile", [(i, (i + 1) % tiles) for i in range(tiles)])
    above = lax.ppermute(first, "tile", [((i + 1) % tiles, i) for i in range(tiles)])
    got = lax.all_to_all(sent, "tile", 0, 0, tiled=True)

    state_shape = jax.ShapeDtypeStruct((FIELDS, WIDE, 2, 32, 128), f32)
    coef_shape = jax.ShapeDtypeStruct((2, WIDE, 2, LEVELS, 128), f32)
    surface = pl.pallas_call(
        surface_kernel,
        out_shape=jax.ShapeDtypeStruct((4, WIDE, 2, 8, 128), f32),
        in_specs=[smem, vmem],
        out_specs=vmem,
        scratch_shapes=[pltpu.VMEM((128, ALONG), f32)],
        compiler_params=pltpu.CompilerParams(vmem_limit_bytes=4 << 20),
        cost_estimate=pl.CostEstimate(flops=10**9, bytes_accessed=10**6, transcendentals=0),
        name="surface",
    )(place, got)
    one, two, coef = pl.pallas_call(
        inner_kernel,
        out_shape=(state_shape, state_shape, coef_shape),
        in_specs=[smem, vmem, vmem, vmem],
        out_specs=(vmem,) * 3,
        compiler_params=pltpu.CompilerParams(vmem_limit_bytes=4 << 20),
        cost_estimate=pl.CostEstimate(flops=10**9, bytes_accessed=10**6, transcendentals=0),
        name="inner",
    )(omega, as_lines(adjoint_start), as_lines(conductivity), surface)

    adjoint, term, *_ = pl.pallas_call(
        functools.partial(outer_kernel, groups),
        out_shape=(
            jax.ShapeDtypeStruct((LINES, 128), f32),
            jax.ShapeDtypeStruct((LEVELS * WIDE, 128), f32),
            state_shape,
            state_shape,
            coef_shape,
        ),
        in_specs=[smem, smem] + [vmem] * 7,
        out_specs=(vmem,) * 5,
        input_output_aliases={4: 2, 5: 3, 6: 4},
        compiler_params=pltpu.CompilerParams(vmem_limit_bytes=4 << 20),
        name="outer",
    )(omega, place, below, above, one, two, coef, surface, as_lines(forward_field))

    terms = lax.all_to_all(term.reshape(groups, -1, 128), "freq", 0, 0, tiled=True)
    gradient = from_lines(terms.sum(axis=0))
    adjoint = pl.pallas_call(
        store_kernel,
        out_shape=jax.ShapeDtypeStruct((LINES, 128), f32),
        in_specs=[vmem],
        out_specs=far,
        scratch_shapes=[pltpu.SemaphoreType.DMA((8,))],
        compiler_params=pltpu.CompilerParams(vmem_limit_bytes=1 << 20),
        name="store",
    )(adjoint)
    return (from_lines(adjoint).reshape(adjoint_start.shape), gradient)


def solution(mesh):
    return jax.shard_map(
        body,
        mesh=mesh,
        in_specs=(
            P("freq"),
            P(None, "tile", None),
            P("freq", None, None, None, "tile", None),
            P("freq", None, None, None, "tile", None),
            P("freq", None, None, "tile"),
            P("tile", None),
            P("tile"),
        ),
        out_specs=(P("freq", None, None, None, "tile", None), P("freq", "tile", None)),
        check_vma=False,
    )
```

```python
import functools
import math

import jax
import jax.numpy as jnp
from jax import lax
from jax.experimental import pallas as pl
from jax.experimental.pallas import tpu as pltpu
from jax.sharding import PartitionSpec as P

SWEEPS = 4
DAMPING = 0.7
DIAGONAL = 5.0
ROWS = 8
HALF = 4
WIDE = 16
LEVELS = 16
ALONG = 256
FIELDS = 6
KINDS = FIELDS + 1
LINES = FIELDS * LEVELS * WIDE
HALO = HALF * KINDS * 2 * LEVELS
f32 = jnp.float32


def as_lines(planes):
    return planes.reshape(-1, ROWS, 2, 128).transpose(0, 2, 1, 3).reshape(-1, 128)


def from_lines(lines):
    return lines.reshape(-1, 2, ROWS, 128).transpose(0, 2, 1, 3).reshape(-1, ROWS, ALONG)


def pack_kernel(field_hbm, sigma_hbm, first_hbm, last_hbm, field_ref, sigma_ref, first_ref, last_ref, in_sems, out_sems):
    size = LEVELS * WIDE
    block = HALF * 2 * LEVELS
    pairs = [
        (field_hbm.at[pl.ds(kind * size, size)], field_ref.at[pl.ds(kind * size, size)])
        for kind in range(FIELDS)
    ]
    pairs.append((sigma_hbm, sigma_ref))
    copies = [
        pltpu.make_async_copy(source, target, in_sems.at[which]) for which, (source, target) in enumerate(pairs)
    ]
    for copy in copies:
        copy.start()
    sends = []
    for kind in range(KINDS):
        copies[kind].wait()
        source, base = (field_ref, kind * LEVELS) if kind < FIELDS else (sigma_ref, 0)
        for x in range(ROWS):
            target = first_ref if x < HALF else last_ref
            for side in range(2):
                for part in range(2):
                    start = (base + 8 * part) * WIDE + side * 8 + x
                    place = ((kind * HALF + x % HALF) * 2 + side) * LEVELS + 8 * part
                    target[place : place + 8] = source[pl.ds(start, 8, stride=WIDE), :]
        rows = pl.ds(kind * block, block)
        for which, (source, target) in enumerate(((first_ref, first_hbm), (last_ref, last_hbm))):
            copy = pltpu.make_async_copy(source.at[rows], target.at[rows], out_sems.at[2 * kind + which])
            copy.start()
            sends.append(copy)
    for copy in sends:
        copy.wait()


def lists_kernel(data_hbm, owner_hbm, cell_hbm, sent_hbm, data_ref, owner_ref, cell_ref, block_ref, in_sems, out_sems):
    copies = [
        pltpu.make_async_copy(source, target, in_sems.at[which])
        for which, (source, target) in enumerate(
            ((data_hbm, data_ref), (owner_hbm, owner_ref), (cell_hbm, cell_ref))
        )
    ]
    for copy in copies:
        copy.start()
    for copy in copies:
        copy.wait()
    for chunk in range(block_ref.shape[0] // 6):
        lanes = slice(128 * chunk, 128 * chunk + 128)
        row = 6 * chunk
        block_ref[row : row + 2] = data_ref[0, :, lanes]
        block_ref[row + 2 : row + 4] = data_ref[1, :, lanes]
        block_ref[row + 4 : row + 5] = owner_ref[:, lanes].astype(f32)
        block_ref[row + 5 : row + 6] = cell_ref[:, lanes].astype(f32)
    sends = [
        pltpu.make_async_copy(block_ref, sent_hbm.at[tile], out_sems.at[tile]) for tile in range(sent_hbm.shape[0])
    ]
    for copy in sends:
        copy.start()
    for copy in sends:
        copy.wait()


def store_kernel(value_ref, out_hbm, sems):
    count = sems.shape[0]
    size = value_ref.shape[0] // count
    copies = [
        pltpu.make_async_copy(
            value_ref.at[pl.ds(size * which, size)], out_hbm.at[pl.ds(size * which, size)], sems.at[which]
        )
        for which in range(count)
    ]
    for copy in copies:
        copy.start()
    for copy in copies:
        copy.wait()


def quarters(place_ref, below_ref, above_ref):
    tile, tiles = place_ref[0], place_ref[1]
    return ((0, below_ref, tile > 0), (HALF + ROWS, above_ref, tile < tiles - 1))


def packed(ref, x, kind, side, part):
    start = ((kind * HALF + x) * 2 + side) * LEVELS + 8 * part
    return ref[pl.ds(pl.multiple_of(start, 8), 8), :]


def set_weights(coef, omega, value, at, side, part, inside=None):
    value = value * omega
    scale = DAMPING / (DIAGONAL * DIAGONAL + value * value)
    if inside is not None:
        scale = jnp.where(inside, scale, 0.0)
    coef[0, at, side, 8 * part : 8 * part + 8] = DIAGONAL * scale
    coef[1, at, side, 8 * part : 8 * part + 8] = value * scale


def y_sum(ahead, behind):
    lane = lax.broadcasted_iota(jnp.int32, (8, 128), 1)
    lane_last, lane_first = lane < 127, lane > 0
    left, right = (pltpu.roll(piece, 127, 1) for piece in ahead)
    low, high = (pltpu.roll(piece, 1, 1) for piece in behind)
    return [
        jnp.where(lane_last, left, right) + jnp.where(lane_first, low, 0.0),
        jnp.where(lane_last, right, 0.0) + jnp.where(lane_first, high, low),
    ]


def advance(x, source, coef, emit, surface_ref=None, parts=(0, 1)):
    for part in parts:
        row = 8 + 8 * part
        off, old = [], []
        for half in range(2):
            ahead, behind, rest = ([], [], []), ([], [], []), ([], [], [])
            for side in range(2):

                def at(comp, dx=0, dz=0, side=side, half=half):
                    return source[3 * half + comp, x + dx, side, row + dz : row + dz + 8]

                u, v, w = at(0), at(1), at(2)
                old.append((u, v, w))
                up, down = at(0, 1), at(0, -1)
                dxu, nxu = up - down, up + down
                up, down = at(1, 1), at(1, -1)
                dxv, nxv = up - down, up + down
                up, down = at(1, 0, 1), at(1, 0, -1)
                dzv, nzv = up - down, up + down
                up, down = at(2, 0, 1), at(2, 0, -1)
                dzw, nzw = up - down, up + down
                nxw = at(2, 1) + at(2, -1)
                nzu = at(0, 0, 1) + at(0, 0, -1)
                ddw = (at(2, 1, 1) - at(2, 1, -1)) - (at(2, -1, 1) - at(2, -1, -1))
                ddu = (at(0, 1, 1) - at(0, 1, -1)) - (at(0, -1, 1) - at(0, -1, -1))
                for comp, (middle, slope) in enumerate(
                    ((u, 0.125 * dxv), (0.5 * v, 0.125 * (dxu + dzw)), (w, 0.125 * dzv))
                ):
                    ahead[comp].append(middle - slope)
                    behind[comp].append(middle + slope)
                rest[0].append((0.5 * nxu + nzu) - 0.125 * ddw)
                rest[1].append(nxv + nzv)
                rest[2].append((0.5 * nzw + nxw) - 0.125 * ddu)
            for comp in range(3):
                sums = y_sum(ahead[comp], behind[comp])
                value = [rest[comp][side] + sums[side] for side in range(2)]
                if part == 0 and comp < 2 and surface_ref is not None:
                    value = [value[side] + surface_ref[2 * half + comp, x, side] for side in range(2)]
                off.append(value)
        for side in range(2):
            c1 = coef[0, x, side, 8 * part : 8 * part + 8]
            c2 = coef[1, x, side, 8 * part : 8 * part + 8]
            news = []
            for comp in range(3):
                re, im = off[comp][side], off[3 + comp][side]
                new_re = (1.0 - DAMPING) * old[side][comp] + (c1 * re - c2 * im)
                new_im = (1.0 - DAMPING) * old[2 + side][comp] + (c2 * re + c1 * im)
                news.append((new_re, new_im))
            emit(x, side, part, news)


def keep_in(target):
    def emit(x, side, part, news):
        for comp, (new_re, new_im) in enumerate(news):
            target[comp, x, side, 8 + 8 * part : 16 + 8 * part] = new_re
            target[3 + comp, x, side, 8 + 8 * part : 16 + 8 * part] = new_im

    return emit


def source_kernel(
    pairs_all, omega_ref, place_ref, lists_ref, coef, forward_ref, out_in, term_in,
    out_ref, term_ref, acc_ref, surface_ref, three, four,
):
    scale = omega_ref[0] * (1.0 / math.sqrt(pairs_all))
    start = place_ref[0] * ROWS - HALF
    sources = lists_ref.shape[0]
    chunks = lists_ref.shape[1] // 6
    row = lax.broadcasted_iota(jnp.int32, (WIDE, 128), 0)
    along = lax.broadcasted_iota(jnp.int32, (ALONG, 128), 0)
    acc_ref[...] = jnp.zeros_like(acc_ref)

    def step(source, carry):
        lefts, rights = [], []
        for chunk in range(chunks):
            block = lists_ref[source, 6 * chunk : 6 * chunk + 6]
            owner = block[4:5].astype(jnp.int32)
            cell = block[5:6].astype(jnp.int32)
            here = owner * ROWS + (cell >> 8) - start == row
            high = block[0:4].astype(jnp.bfloat16).astype(f32)
            rest = block[0:4] - high
            parts = []
            for which in range(4):
                for value in (high, rest):
                    parts.append(jnp.where(here, value[which : which + 1], 0.0).astype(jnp.bfloat16))
            lefts.append(jnp.concatenate(parts, axis=0))
            rights.append(jnp.where(along == (cell & 255), 1.0, 0.0).astype(jnp.bfloat16))
        acc_ref[...] += lax.dot_general(
            jnp.concatenate(lefts, axis=1),
            jnp.concatenate(rights, axis=1),
            (((1,), (1,)), ((), ())),
            preferred_element_type=f32,
        )
        return carry

    lax.fori_loop(0, sources, step, 0, unroll=8)
    top = lax.broadcasted_iota(jnp.int32, (8, 128), 0) == 0
    for which in range(4):
        total = acc_ref[32 * which : 32 * which + 16] + acc_ref[32 * which + 16 : 32 * which + 32]
        for x in range(WIDE):
            for side in range(2):
                line = total[x : x + 1, 128 * side : 128 * side + 128]
                surface_ref[which, x, side] = jnp.where(top, line, 0.0)

    zero = jnp.zeros((8, 128), f32)

    def clear(x, carry):
        for side in range(2):
            for field in range(FIELDS):
                for buffer in (three, four):
                    buffer[field, x, side, 0:8] = zero
                    buffer[field, x, side, 16:24] = zero
            three[2, x, side, 8:16] = zero
            three[5, x, side, 8:16] = zero
        return carry

    lax.fori_loop(1, WIDE - 1, clear, 0, unroll=2)
    for x in range(1, WIDE - 1):
        for side in range(2):
            c1, c2 = coef[0, x, side, 0:8], coef[1, x, side, 0:8]
            for comp in range(2):
                re, im = surface_ref[comp, x, side], surface_ref[2 + comp, x, side]
                three[comp, x, side, 8:16] = c1 * re - c2 * im
                three[3 + comp, x, side, 8:16] = c2 * re + c1 * im

    def add_out(x, side, part, news):
        base = side * 8 + x - HALF
        total = None
        for comp, (new_re, new_im) in enumerate(news):
            re_at = pl.ds(comp * LEVELS * WIDE + base, 8, stride=WIDE)
            im_at = pl.ds((3 + comp) * LEVELS * WIDE + base, 8, stride=WIDE)
            out_ref[re_at, :] = out_ref[re_at, :] + new_re
            out_ref[im_at, :] = out_ref[im_at, :] + new_im
            piece = forward_ref[re_at, :] * new_im + forward_ref[im_at, :] * new_re
            total = piece if total is None else total + piece
        at = pl.ds(base, 8, stride=WIDE)
        term_ref[at, :] = term_in[at, :] + total * scale

    half = LEVELS * WIDE // 2
    term_ref[half : 2 * half] = term_in[half : 2 * half]
    buffers = (four, three)
    for sweep in range(1, SWEEPS):
        source, target = buffers[sweep % 2], buffers[1 - sweep % 2]
        emit = add_out if sweep == SWEEPS - 1 else keep_in(target)

        def slices(step, carry, source=source, emit=emit, begin=1 + sweep):
            for x in range(2):
                advance(begin + 2 * step + x, source, coef, emit, surface_ref, (0,))
            return carry

        lax.fori_loop(0, (WIDE - 2 - 2 * sweep) // 2, slices, 0, unroll=(3, 5, 4)[sweep - 1])


def inner_kernel(omega_ref, field_ref, sigma_ref, one, two, coef):
    omega = omega_ref[0]
    zero = jnp.zeros((8, 128), f32)

    def clear(x, carry):
        for side in range(2):
            for field in range(FIELDS):
                for buffer in (one, two):
                    buffer[field, x, side, 0:8] = zero
                    buffer[field, x, side, 24:32] = zero
        return carry

    lax.fori_loop(0, WIDE, clear, 0)

    def fill(x, carry):
        for side in range(2):
            for part in range(2):
                for field in range(FIELDS):
                    at = (field * LEVELS + 8 * part) * WIDE + side * 8 + x
                    value = field_ref[pl.ds(at, 8, stride=WIDE), :]
                    one[field, HALF + x, side, 8 + 8 * part : 16 + 8 * part] = value
                value = sigma_ref[pl.ds(8 * part * WIDE + side * 8 + x, 8, stride=WIDE), :]
                set_weights(coef, omega, value, HALF + x, side, part)
        return carry

    lax.fori_loop(0, ROWS, fill, 0)

    buffers = (one, two)
    for sweep in range(SWEEPS - 1):
        source, target = buffers[sweep % 2], buffers[1 - sweep % 2]

        def slices(step, carry, source=source, target=target, begin=HALF + 1 + sweep):
            for x in range(2):
                advance(begin + 2 * step + x, source, coef, keep_in(target))
            return carry

        lax.fori_loop(0, ROWS // 2 - 1 - sweep, slices, 0, unroll=ROWS // 2 - 1 - sweep)


def outer_kernel(
    pairs_all,
    omega_ref,
    place_ref,
    below_ref,
    above_ref,
    one_in,
    two_in,
    coef_in,
    forward_ref,
    out_ref,
    term_ref,
    one,
    two,
    coef,
):
    omega = omega_ref[0]
    scale = omega * (1.0 / math.sqrt(pairs_all))

    for base, ref, inside in quarters(place_ref, below_ref, above_ref):

        def fill(x, carry, base=base, ref=ref, inside=inside):
            for side in range(2):
                for part in range(2):
                    for field in range(FIELDS):
                        value = jnp.where(inside, packed(ref, x, field, side, part), 0.0)
                        one[field, base + x, side, 8 + 8 * part : 16 + 8 * part] = value
                    value = packed(ref, x, FIELDS, side, part)
                    set_weights(coef, omega, value, base + x, side, part, inside)
            return carry

        lax.fori_loop(0, HALF, fill, 0)

    def give_out(x, side, part, news):
        base = side * 8 + x - HALF
        total = None
        for comp, (new_re, new_im) in enumerate(news):
            re_at = pl.ds((comp * LEVELS + 8 * part) * WIDE + base, 8, stride=WIDE)
            im_at = pl.ds(((3 + comp) * LEVELS + 8 * part) * WIDE + base, 8, stride=WIDE)
            out_ref[re_at, :] = new_re
            out_ref[im_at, :] = new_im
            piece = forward_ref[re_at, :] * new_im + forward_ref[im_at, :] * new_re
            total = piece if total is None else total + piece
        term_ref[pl.ds(8 * part * WIDE + base, 8, stride=WIDE), :] = total * scale

    buffers = (one, two)
    for sweep in range(SWEEPS):
        source, target = buffers[sweep % 2], buffers[1 - sweep % 2]
        emit = give_out if sweep == SWEEPS - 1 else keep_in(target)

        def slices(step, carry, source=source, emit=emit, sweep=sweep):
            for x in range(2):
                advance(1 + sweep + 2 * step + x, source, coef, emit)
                advance(WIDE - 1 - HALF - sweep + 2 * step + x, source, coef, emit)
            return carry

        lax.fori_loop(0, HALF // 2, slices, 0, unroll=2)


def body(
    omega, conductivity, forward_field, adjoint_start, station_data, station_owner, station_cell
):
    listed = station_cell.shape[0]
    tiles = lax.axis_size("tile")
    groups = lax.axis_size("freq")
    place = jnp.stack([lax.axis_index("tile"), jnp.int32(tiles)])

    vmem = pl.BlockSpec(memory_space=pltpu.VMEM)
    smem = pl.BlockSpec(memory_space=pltpu.SMEM)

    far = pl.BlockSpec(memory_space=pltpu.HBM)
    sent = pl.pallas_call(
        lists_kernel,
        out_shape=jax.ShapeDtypeStruct((tiles, 6 * listed // 128, 128), f32),
        in_specs=[far] * 3,
        out_specs=far,
        scratch_shapes=[
            pltpu.VMEM((2, 2, listed), f32),
            pltpu.VMEM((1, listed), jnp.int32),
            pltpu.VMEM((1, listed), jnp.int32),
            pltpu.VMEM((6 * listed // 128, 128), f32),
            pltpu.SemaphoreType.DMA((3,)),
            pltpu.SemaphoreType.DMA((tiles,)),
        ],
        cost_estimate=pl.CostEstimate(flops=10**9, bytes_accessed=10**6, transcendentals=0),
        name="lists",
    )(station_data.reshape(2, 2, listed), station_owner.reshape(1, listed), station_cell.reshape(1, listed))
    first, last = pl.pallas_call(
        pack_kernel,
        out_shape=(
            jax.ShapeDtypeStruct((HALO, 128), f32),
            jax.ShapeDtypeStruct((HALO, 128), f32),
        ),
        in_specs=[far] * 2,
        out_specs=(far, far),
        scratch_shapes=[
            pltpu.VMEM((LINES, 128), f32),
            pltpu.VMEM((LEVELS * WIDE, 128), f32),
            pltpu.VMEM((HALO, 128), f32),
            pltpu.VMEM((HALO, 128), f32),
            pltpu.SemaphoreType.DMA((KINDS,)),
            pltpu.SemaphoreType.DMA((2 * KINDS,)),
        ],
        name="pack",
    )(as_lines(adjoint_start), as_lines(conductivity))
    below = lax.ppermute(last, "tile", [(i, (i + 1) % tiles) for i in range(tiles)])
    above = lax.ppermute(first, "tile", [((i + 1) % tiles, i) for i in range(tiles)])
    got = lax.all_to_all(sent, "tile", 0, 0, tiled=True)

    state_shape = jax.ShapeDtypeStruct((FIELDS, WIDE, 2, 32, 128), f32)
    coef_shape = jax.ShapeDtypeStruct((2, WIDE, 2, LEVELS, 128), f32)
    cost = pl.CostEstimate(flops=10**9, bytes_accessed=10**6, transcendentals=0)
    one, two, coef = pl.pallas_call(
        inner_kernel,
        out_shape=(state_shape, state_shape, coef_shape),
        in_specs=[smem, vmem, vmem],
        out_specs=(vmem,) * 3,
        compiler_params=pltpu.CompilerParams(vmem_limit_bytes=4 << 20),
        cost_estimate=cost,
        name="inner",
    )(omega, as_lines(adjoint_start), as_lines(conductivity))

    lines_shape = jax.ShapeDtypeStruct((LINES, 128), f32)
    term_shape = jax.ShapeDtypeStruct((LEVELS * WIDE, 128), f32)
    forward = as_lines(forward_field)
    adjoint, term, _, _, coef = pl.pallas_call(
        functools.partial(outer_kernel, groups),
        out_shape=(lines_shape, term_shape, state_shape, state_shape, coef_shape),
        in_specs=[smem, smem] + [vmem] * 6,
        out_specs=(vmem,) * 5,
        input_output_aliases={4: 2, 5: 3, 6: 4},
        compiler_params=pltpu.CompilerParams(vmem_limit_bytes=4 << 20),
        cost_estimate=cost,
        name="outer",
    )(omega, place, below, above, one, two, coef, forward)

    adjoint, term = pl.pallas_call(
        functools.partial(source_kernel, groups),
        out_shape=(lines_shape, term_shape),
        in_specs=[smem, smem] + [vmem] * 5,
        out_specs=(vmem,) * 2,
        scratch_shapes=[
            pltpu.VMEM((128, ALONG), f32),
            pltpu.VMEM((4, WIDE, 2, 8, 128), f32),
            pltpu.VMEM((FIELDS, WIDE, 2, 24, 128), f32),
            pltpu.VMEM((FIELDS, WIDE, 2, 24, 128), f32),
        ],
        input_output_aliases={5: 0},
        compiler_params=pltpu.CompilerParams(vmem_limit_bytes=10 << 20),
        cost_estimate=cost,
        name="source",
    )(omega, place, got, coef, forward, adjoint, term)

    terms = lax.all_to_all(term.reshape(groups, -1, 128), "freq", 0, 0, tiled=True)
    gradient = from_lines(terms.sum(axis=0))
    adjoint = pl.pallas_call(
        store_kernel,
        out_shape=jax.ShapeDtypeStruct((LINES, 128), f32),
        in_specs=[vmem],
        out_specs=far,
        scratch_shapes=[pltpu.SemaphoreType.DMA((8,))],
        compiler_params=pltpu.CompilerParams(vmem_limit_bytes=1 << 20),
        name="store",
    )(adjoint)
    return (from_lines(adjoint).reshape(adjoint_start.shape), gradient)


def solution(mesh):
    return jax.shard_map(
        body,
        mesh=mesh,
        in_specs=(
            P("freq"),
            P(None, "tile", None),
            P("freq", None, None, None, "tile", None),
            P("freq", None, None, None, "tile", None),
            P("freq", None, None, "tile"),
            P("tile", None),
            P("tile"),
        ),
        out_specs=(P("freq", None, None, None, "tile", None), P("freq", "tile", None)),
        check_vma=False,
    )
```

```python
import functools
import math

import jax
import jax.numpy as jnp
from jax import lax
from jax.experimental import pallas as pl
from jax.experimental.pallas import tpu as pltpu
from jax.sharding import PartitionSpec as P

SWEEPS = 4
DAMPING = 0.7
DIAGONAL = 5.0
ROWS = 8
HALF = 4
WIDE = 16
LEVELS = 16
ALONG = 256
FIELDS = 6
KINDS = FIELDS + 1
LINES = FIELDS * LEVELS * WIDE
HALO = HALF * KINDS * 2 * LEVELS
f32 = jnp.float32


def as_lines(planes):
    return planes.reshape(-1, ROWS, 2, 128).transpose(0, 2, 1, 3).reshape(-1, 128)


def from_lines(lines):
    return lines.reshape(-1, 2, ROWS, 128).transpose(0, 2, 1, 3).reshape(-1, ROWS, ALONG)


def pack_kernel(
    data_hbm, owner_hbm, cell_hbm, field_hbm, sigma_hbm, sent_hbm, first_hbm, last_hbm,
    data_ref, owner_ref, cell_ref, field_ref, sigma_ref, list_ref, first_ref, last_ref,
    in_sems, list_sems, out_sems,
):
    size = LEVELS * WIDE
    block = HALF * 2 * LEVELS
    pairs = [(data_hbm, data_ref), (owner_hbm, owner_ref), (cell_hbm, cell_ref)]
    pairs += [
        (field_hbm.at[pl.ds(kind * size, size)], field_ref.at[pl.ds(kind * size, size)])
        for kind in range(FIELDS)
    ]
    pairs.append((sigma_hbm, sigma_ref))
    copies = [
        pltpu.make_async_copy(source, target, in_sems.at[which]) for which, (source, target) in enumerate(pairs)
    ]
    for copy in copies:
        copy.start()
    for copy in copies[:3]:
        copy.wait()
    for chunk in range(list_ref.shape[0] // 6):
        lanes = slice(128 * chunk, 128 * chunk + 128)
        row = 6 * chunk
        list_ref[row : row + 2] = data_ref[0, :, lanes]
        list_ref[row + 2 : row + 4] = data_ref[1, :, lanes]
        list_ref[row + 4 : row + 5] = owner_ref[:, lanes].astype(f32)
        list_ref[row + 5 : row + 6] = cell_ref[:, lanes].astype(f32)
    sends = [
        pltpu.make_async_copy(list_ref, sent_hbm.at[tile], list_sems.at[tile]) for tile in range(sent_hbm.shape[0])
    ]
    for copy in sends:
        copy.start()
    for kind in range(KINDS):
        copies[3 + kind].wait()
        source, base = (field_ref, kind * LEVELS) if kind < FIELDS else (sigma_ref, 0)
        for x in range(ROWS):
            target = first_ref if x < HALF else last_ref
            for side in range(2):
                for part in range(2):
                    start = (base + 8 * part) * WIDE + side * 8 + x
                    place = ((kind * HALF + x % HALF) * 2 + side) * LEVELS + 8 * part
                    target[place : place + 8] = source[pl.ds(start, 8, stride=WIDE), :]
        rows = pl.ds(kind * block, block)
        for which, (source, target) in enumerate(((first_ref, first_hbm), (last_ref, last_hbm))):
            copy = pltpu.make_async_copy(source.at[rows], target.at[rows], out_sems.at[2 * kind + which])
            copy.start()
            sends.append(copy)
    for copy in sends:
        copy.wait()


def store_kernel(value_ref, out_hbm, sems):
    count = sems.shape[0]
    size = value_ref.shape[0] // count
    copies = [
        pltpu.make_async_copy(
            value_ref.at[pl.ds(size * which, size)], out_hbm.at[pl.ds(size * which, size)], sems.at[which]
        )
        for which in range(count)
    ]
    for copy in copies:
        copy.start()
    for copy in copies:
        copy.wait()


def quarters(place_ref, below_ref, above_ref):
    tile, tiles = place_ref[0], place_ref[1]
    return ((0, below_ref, tile > 0), (HALF + ROWS, above_ref, tile < tiles - 1))


def packed(ref, x, kind, side, part):
    start = ((kind * HALF + x) * 2 + side) * LEVELS + 8 * part
    return ref[pl.ds(pl.multiple_of(start, 8), 8), :]


def set_weights(coef, omega, value, at, side, part, inside=None):
    value = value * omega
    scale = DAMPING / (DIAGONAL * DIAGONAL + value * value)
    if inside is not None:
        scale = jnp.where(inside, scale, 0.0)
    coef[0, at, side, 8 * part : 8 * part + 8] = DIAGONAL * scale
    coef[1, at, side, 8 * part : 8 * part + 8] = value * scale


def y_sum(ahead, behind):
    lane = lax.broadcasted_iota(jnp.int32, (8, 128), 1)
    lane_last, lane_first = lane < 127, lane > 0
    left, right = (pltpu.roll(piece, 127, 1) for piece in ahead)
    low, high = (pltpu.roll(piece, 1, 1) for piece in behind)
    return [
        jnp.where(lane_last, left, right) + jnp.where(lane_first, low, 0.0),
        jnp.where(lane_last, right, 0.0) + jnp.where(lane_first, high, low),
    ]


def advance(x, source, coef, emit, surface_ref=None, parts=(0, 1)):
    for part in parts:
        row = 8 + 8 * part
        off, old = [], []
        for half in range(2):
            ahead, behind, rest = ([], [], []), ([], [], []), ([], [], [])
            for side in range(2):

                def at(comp, dx=0, dz=0, side=side, half=half):
                    return source[3 * half + comp, x + dx, side, row + dz : row + dz + 8]

                u, v, w = at(0), at(1), at(2)
                old.append((u, v, w))
                up, down = at(0, 1), at(0, -1)
                dxu, nxu = up - down, up + down
                up, down = at(1, 1), at(1, -1)
                dxv, nxv = up - down, up + down
                up, down = at(1, 0, 1), at(1, 0, -1)
                dzv, nzv = up - down, up + down
                up, down = at(2, 0, 1), at(2, 0, -1)
                dzw, nzw = up - down, up + down
                nxw = at(2, 1) + at(2, -1)
                nzu = at(0, 0, 1) + at(0, 0, -1)
                ddw = (at(2, 1, 1) - at(2, 1, -1)) - (at(2, -1, 1) - at(2, -1, -1))
                ddu = (at(0, 1, 1) - at(0, 1, -1)) - (at(0, -1, 1) - at(0, -1, -1))
                for comp, (middle, slope) in enumerate(
                    ((u, 0.125 * dxv), (0.5 * v, 0.125 * (dxu + dzw)), (w, 0.125 * dzv))
                ):
                    ahead[comp].append(middle - slope)
                    behind[comp].append(middle + slope)
                rest[0].append((0.5 * nxu + nzu) - 0.125 * ddw)
                rest[1].append(nxv + nzv)
                rest[2].append((0.5 * nzw + nxw) - 0.125 * ddu)
            for comp in range(3):
                sums = y_sum(ahead[comp], behind[comp])
                value = [rest[comp][side] + sums[side] for side in range(2)]
                if part == 0 and comp < 2 and surface_ref is not None:
                    value = [value[side] + surface_ref[2 * half + comp, x, side] for side in range(2)]
                off.append(value)
        for side in range(2):
            c1 = coef[0, x, side, 8 * part : 8 * part + 8]
            c2 = coef[1, x, side, 8 * part : 8 * part + 8]
            news = []
            for comp in range(3):
                re, im = off[comp][side], off[3 + comp][side]
                new_re = (1.0 - DAMPING) * old[side][comp] + (c1 * re - c2 * im)
                new_im = (1.0 - DAMPING) * old[2 + side][comp] + (c2 * re + c1 * im)
                news.append((new_re, new_im))
            emit(x, side, part, news)


def keep_in(target):
    def emit(x, side, part, news):
        for comp, (new_re, new_im) in enumerate(news):
            target[comp, x, side, 8 + 8 * part : 16 + 8 * part] = new_re
            target[3 + comp, x, side, 8 + 8 * part : 16 + 8 * part] = new_im

    return emit


def source_kernel(
    pairs_all, omega_ref, place_ref, lists_ref, coef, forward_ref, out_in, term_in,
    out_ref, term_ref, acc_ref, surface_ref, three, four,
):
    scale = omega_ref[0] * (1.0 / math.sqrt(pairs_all))
    start = place_ref[0] * ROWS - HALF
    sources = lists_ref.shape[0]
    chunks = lists_ref.shape[1] // 6
    row = lax.broadcasted_iota(jnp.int32, (WIDE, 128), 0)
    along = lax.broadcasted_iota(jnp.int32, (ALONG, 128), 0)
    acc_ref[...] = jnp.zeros_like(acc_ref)

    def step(source, carry):
        lefts, rights = [], []
        for chunk in range(chunks):
            block = lists_ref[source, 6 * chunk : 6 * chunk + 6]
            owner = block[4:5].astype(jnp.int32)
            cell = block[5:6].astype(jnp.int32)
            here = owner * ROWS + (cell >> 8) - start == row
            high = block[0:4].astype(jnp.bfloat16).astype(f32)
            rest = block[0:4] - high
            parts = []
            for which in range(4):
                for value in (high, rest):
                    parts.append(jnp.where(here, value[which : which + 1], 0.0).astype(jnp.bfloat16))
            lefts.append(jnp.concatenate(parts, axis=0))
            rights.append(jnp.where(along == (cell & 255), 1.0, 0.0).astype(jnp.bfloat16))
        acc_ref[...] += lax.dot_general(
            jnp.concatenate(lefts, axis=1),
            jnp.concatenate(rights, axis=1),
            (((1,), (1,)), ((), ())),
            preferred_element_type=f32,
        )
        return carry

    lax.fori_loop(0, sources, step, 0, unroll=16)
    top = lax.broadcasted_iota(jnp.int32, (8, 128), 0) == 0
    for which in range(4):
        total = acc_ref[32 * which : 32 * which + 16] + acc_ref[32 * which + 16 : 32 * which + 32]
        for x in range(WIDE):
            for side in range(2):
                line = total[x : x + 1, 128 * side : 128 * side + 128]
                surface_ref[which, x, side] = jnp.where(top, line, 0.0)

    zero = jnp.zeros((8, 128), f32)

    def clear(x, carry):
        for side in range(2):
            for field in range(FIELDS):
                for buffer in (three, four):
                    buffer[field, x, side, 0:8] = zero
                    buffer[field, x, side, 16:24] = zero
            three[2, x, side, 8:16] = zero
            three[5, x, side, 8:16] = zero
        return carry

    lax.fori_loop(1, WIDE - 1, clear, 0, unroll=2)
    for x in range(1, WIDE - 1):
        for side in range(2):
            c1, c2 = coef[0, x, side, 0:8], coef[1, x, side, 0:8]
            for comp in range(2):
                re, im = surface_ref[comp, x, side], surface_ref[2 + comp, x, side]
                three[comp, x, side, 8:16] = c1 * re - c2 * im
                three[3 + comp, x, side, 8:16] = c2 * re + c1 * im

    def add_out(x, side, part, news):
        base = side * 8 + x - HALF
        total = None
        for comp, (new_re, new_im) in enumerate(news):
            re_at = pl.ds(comp * LEVELS * WIDE + base, 8, stride=WIDE)
            im_at = pl.ds((3 + comp) * LEVELS * WIDE + base, 8, stride=WIDE)
            out_ref[re_at, :] = out_ref[re_at, :] + new_re
            out_ref[im_at, :] = out_ref[im_at, :] + new_im
            piece = forward_ref[re_at, :] * new_im + forward_ref[im_at, :] * new_re
            total = piece if total is None else total + piece
        at = pl.ds(base, 8, stride=WIDE)
        term_ref[at, :] = term_in[at, :] + total * scale

    half = LEVELS * WIDE // 2
    term_ref[half : 2 * half] = term_in[half : 2 * half]
    buffers = (four, three)
    for sweep in range(1, SWEEPS):
        source, target = buffers[sweep % 2], buffers[1 - sweep % 2]
        emit = add_out if sweep == SWEEPS - 1 else keep_in(target)

        def slices(step, carry, source=source, emit=emit, begin=1 + sweep):
            for x in range(2):
                advance(begin + 2 * step + x, source, coef, emit, surface_ref, (0,))
            return carry

        lax.fori_loop(0, (WIDE - 2 - 2 * sweep) // 2, slices, 0, unroll=(3, 5, 4)[sweep - 1])


def inner_kernel(omega_ref, field_ref, sigma_ref, one, two, coef):
    omega = omega_ref[0]
    zero = jnp.zeros((8, 128), f32)

    def clear(x, carry):
        for side in range(2):
            for field in range(FIELDS):
                for buffer in (one, two):
                    buffer[field, x, side, 0:8] = zero
                    buffer[field, x, side, 24:32] = zero
        return carry

    lax.fori_loop(0, WIDE, clear, 0)

    def fill(x, carry):
        for side in range(2):
            for part in range(2):
                for field in range(FIELDS):
                    at = (field * LEVELS + 8 * part) * WIDE + side * 8 + x
                    value = field_ref[pl.ds(at, 8, stride=WIDE), :]
                    one[field, HALF + x, side, 8 + 8 * part : 16 + 8 * part] = value
                value = sigma_ref[pl.ds(8 * part * WIDE + side * 8 + x, 8, stride=WIDE), :]
                set_weights(coef, omega, value, HALF + x, side, part)
        return carry

    lax.fori_loop(0, ROWS, fill, 0)

    buffers = (one, two)
    for sweep in range(SWEEPS - 1):
        source, target = buffers[sweep % 2], buffers[1 - sweep % 2]

        def slices(step, carry, source=source, target=target, begin=HALF + 1 + sweep):
            for x in range(2):
                advance(begin + 2 * step + x, source, coef, keep_in(target))
            return carry

        lax.fori_loop(0, ROWS // 2 - 1 - sweep, slices, 0, unroll=ROWS // 2 - 1 - sweep)


def outer_kernel(
    pairs_all,
    omega_ref,
    place_ref,
    below_ref,
    above_ref,
    one_in,
    two_in,
    coef_in,
    forward_ref,
    out_ref,
    term_ref,
    one,
    two,
    coef,
):
    omega = omega_ref[0]
    scale = omega * (1.0 / math.sqrt(pairs_all))

    for base, ref, inside in quarters(place_ref, below_ref, above_ref):

        def fill(x, carry, base=base, ref=ref, inside=inside):
            for side in range(2):
                for part in range(2):
                    for field in range(FIELDS):
                        value = jnp.where(inside, packed(ref, x, field, side, part), 0.0)
                        one[field, base + x, side, 8 + 8 * part : 16 + 8 * part] = value
                    value = packed(ref, x, FIELDS, side, part)
                    set_weights(coef, omega, value, base + x, side, part, inside)
            return carry

        lax.fori_loop(0, HALF, fill, 0)

    def give_out(x, side, part, news):
        base = side * 8 + x - HALF
        total = None
        for comp, (new_re, new_im) in enumerate(news):
            re_at = pl.ds((comp * LEVELS + 8 * part) * WIDE + base, 8, stride=WIDE)
            im_at = pl.ds(((3 + comp) * LEVELS + 8 * part) * WIDE + base, 8, stride=WIDE)
            out_ref[re_at, :] = new_re
            out_ref[im_at, :] = new_im
            piece = forward_ref[re_at, :] * new_im + forward_ref[im_at, :] * new_re
            total = piece if total is None else total + piece
        term_ref[pl.ds(8 * part * WIDE + base, 8, stride=WIDE), :] = total * scale

    buffers = (one, two)
    for sweep in range(SWEEPS):
        source, target = buffers[sweep % 2], buffers[1 - sweep % 2]
        emit = give_out if sweep == SWEEPS - 1 else keep_in(target)

        def slices(step, carry, source=source, emit=emit, sweep=sweep):
            for x in range(2):
                advance(1 + sweep + 2 * step + x, source, coef, emit)
                advance(WIDE - 1 - HALF - sweep + 2 * step + x, source, coef, emit)
            return carry

        lax.fori_loop(0, HALF // 2, slices, 0, unroll=2)


def body(
    omega, conductivity, forward_field, adjoint_start, station_data, station_owner, station_cell
):
    listed = station_cell.shape[0]
    tiles = lax.axis_size("tile")
    groups = lax.axis_size("freq")
    place = jnp.stack([lax.axis_index("tile"), jnp.int32(tiles)])

    vmem = pl.BlockSpec(memory_space=pltpu.VMEM)
    smem = pl.BlockSpec(memory_space=pltpu.SMEM)

    far = pl.BlockSpec(memory_space=pltpu.HBM)
    sent, first, last = pl.pallas_call(
        pack_kernel,
        out_shape=(
            jax.ShapeDtypeStruct((tiles, 6 * listed // 128, 128), f32),
            jax.ShapeDtypeStruct((HALO, 128), f32),
            jax.ShapeDtypeStruct((HALO, 128), f32),
        ),
        in_specs=[far] * 5,
        out_specs=(far,) * 3,
        scratch_shapes=[
            pltpu.VMEM((2, 2, listed), f32),
            pltpu.VMEM((1, listed), jnp.int32),
            pltpu.VMEM((1, listed), jnp.int32),
            pltpu.VMEM((LINES, 128), f32),
            pltpu.VMEM((LEVELS * WIDE, 128), f32),
            pltpu.VMEM((6 * listed // 128, 128), f32),
            pltpu.VMEM((HALO, 128), f32),
            pltpu.VMEM((HALO, 128), f32),
            pltpu.SemaphoreType.DMA((3 + KINDS,)),
            pltpu.SemaphoreType.DMA((tiles,)),
            pltpu.SemaphoreType.DMA((2 * KINDS,)),
        ],
        cost_estimate=pl.CostEstimate(flops=10**9, bytes_accessed=10**6, transcendentals=0),
        name="pack",
    )(
        station_data.reshape(2, 2, listed),
        station_owner.reshape(1, listed),
        station_cell.reshape(1, listed),
        as_lines(adjoint_start),
        as_lines(conductivity),
    )
    below = lax.ppermute(last, "tile", [(i, (i + 1) % tiles) for i in range(tiles)])
    above = lax.ppermute(first, "tile", [((i + 1) % tiles, i) for i in range(tiles)])
    got = lax.all_to_all(sent, "tile", 0, 0, tiled=True)

    state_shape = jax.ShapeDtypeStruct((FIELDS, WIDE, 2, 32, 128), f32)
    coef_shape = jax.ShapeDtypeStruct((2, WIDE, 2, LEVELS, 128), f32)
    cost = pl.CostEstimate(flops=10**9, bytes_accessed=10**6, transcendentals=0)
    one, two, coef = pl.pallas_call(
        inner_kernel,
        out_shape=(state_shape, state_shape, coef_shape),
        in_specs=[smem, vmem, vmem],
        out_specs=(vmem,) * 3,
        compiler_params=pltpu.CompilerParams(vmem_limit_bytes=4 << 20),
        cost_estimate=cost,
        name="inner",
    )(omega, as_lines(adjoint_start), as_lines(conductivity))

    lines_shape = jax.ShapeDtypeStruct((LINES, 128), f32)
    term_shape = jax.ShapeDtypeStruct((LEVELS * WIDE, 128), f32)
    forward = as_lines(forward_field)
    adjoint, term, _, _, coef = pl.pallas_call(
        functools.partial(outer_kernel, groups),
        out_shape=(lines_shape, term_shape, state_shape, state_shape, coef_shape),
        in_specs=[smem, smem] + [vmem] * 6,
        out_specs=(vmem,) * 5,
        input_output_aliases={4: 2, 5: 3, 6: 4},
        compiler_params=pltpu.CompilerParams(vmem_limit_bytes=4 << 20),
        cost_estimate=cost,
        name="outer",
    )(omega, place, below, above, one, two, coef, forward)

    adjoint, term = pl.pallas_call(
        functools.partial(source_kernel, groups),
        out_shape=(lines_shape, term_shape),
        in_specs=[smem, smem] + [vmem] * 5,
        out_specs=(vmem,) * 2,
        scratch_shapes=[
            pltpu.VMEM((128, ALONG), f32),
            pltpu.VMEM((4, WIDE, 2, 8, 128), f32),
            pltpu.VMEM((FIELDS, WIDE, 2, 24, 128), f32),
            pltpu.VMEM((FIELDS, WIDE, 2, 24, 128), f32),
        ],
        input_output_aliases={5: 0},
        compiler_params=pltpu.CompilerParams(vmem_limit_bytes=10 << 20),
        cost_estimate=cost,
        name="source",
    )(omega, place, got, coef, forward, adjoint, term)

    terms = lax.all_to_all(term.reshape(groups, -1, 128), "freq", 0, 0, tiled=True)
    gradient = from_lines(terms.sum(axis=0))
    adjoint = pl.pallas_call(
        store_kernel,
        out_shape=jax.ShapeDtypeStruct((LINES, 128), f32),
        in_specs=[vmem],
        out_specs=far,
        scratch_shapes=[pltpu.SemaphoreType.DMA((8,))],
        compiler_params=pltpu.CompilerParams(vmem_limit_bytes=1 << 20),
        name="store",
    )(adjoint)
    return (from_lines(adjoint).reshape(adjoint_start.shape), gradient)


def solution(mesh):
    return jax.shard_map(
        body,
        mesh=mesh,
        in_specs=(
            P("freq"),
            P(None, "tile", None),
            P("freq", None, None, None, "tile", None),
            P("freq", None, None, None, "tile", None),
            P("freq", None, None, "tile"),
            P("tile", None),
            P("tile"),
        ),
        out_specs=(P("freq", None, None, None, "tile", None), P("freq", "tile", None)),
        check_vma=False,
    )
```
